256 devices in a mesh: leaf: 64 (over y, x, z_hi, core), blk: 4 (over z_lo).
Axes of the slice: x: 4, y: 4, z: 8 (z_hi: 2, z_lo: 4; z = z_hi * 4 + z_lo), core: 2. Of those that a mesh axis runs over, the one named last changes fastest.
Arguments:
- interface: bfloat16 [262144, 512], P(('leaf', 'blk')), may hold values from -6 to 6
- owners: int32 [262144, 1], P(('leaf', 'blk')), may hold values from 0 to 63; in each aligned block of 1024 rows (0 to 1023, 1024 to 2047, ...) at most 32 rows name the same one
- keep_proj: bfloat16 [3, 512, 512], replicated, may hold values from -0.25 to 0.25
- sibling_proj: bfloat16 [3, 512, 512], replicated, may hold values from -0.25 to 0.25
- coupling: bfloat16 [64, 512, 512], P('leaf'), may hold values from -0.25 to 0.25
- pattern: int32 [64, 8, 8], P('leaf'), may hold values 0 or 1
Outputs:
- coupled: bfloat16 [262144, 512], P(('leaf', 'blk'))
The draws below stay inside these ranges and needn't reach their ends.
Inputs may be any that keep to these rules, and one draw needn't show every extreme that they name: `owners`: among the 1024 rows of one device no owner is named by more than 32 rows, a bound that some block reaches.
All inputs are finite; a program needn't handle non-finite values. No bound on the sum of `pattern` on one device may be relied on, other than what follows from the above.
Results may differ from the reference program's by a relative error of at most 0.0075.
Values may be sent and summed in bfloat16 or wider, within the bound.
A program may use at most 64 MiB of HBM per device.

```python
import math
import jax
import jax.numpy as jnp
import numpy as np
from jax import lax

MODES = 512
BS = 64
LEVELS = 3
ROWS = 1024
NBLK = 8
TOTAL = 262144
N_LEAF = 64
N_BLK = 4


def place_ends(entries, stream_key, low, high):
    dims = entries.shape
    index_at = [jax.random.randint(jax.random.fold_in(stream_key, axis), (), 0, dims[axis]) for axis in range(len(dims))]
    entries = entries.at[tuple(index_at)].set(low)
    longest = dims.index(max(dims))
    index_at[longest] = (index_at[longest] + 1) % dims[longest]
    return entries.at[tuple(index_at)].set(high)


def shard_levels(rng, extent, pieces, low, high):
    gain = 1.0
    for dim, shards_of in pieces:
        heights = jax.random.uniform(jax.random.fold_in(jax.random.fold_in(rng, 6), dim), (shards_of,), jnp.float32, low / len(pieces), high / len(pieces))
        gain = gain * jnp.repeat(jnp.exp(heights), extent[dim] // shards_of).reshape((-1,) + (1,) * (len(extent) - 1 - dim))
    return gain


def assign_block(own_key, own, number, rows, count, top, bound, lean):
    ranking = jax.random.permutation(own_key, count)
    crowded, usual = load_shares(count, rows * top, bound, lean, True), load_shares(count, rows * top, bound, lean, False)
    places = jnp.arange(count)

    def named(lengths, rotation):
        used = int((lengths > 0).sum())
        fixed = max(1, used // 4)
        passed = fixed + (places - fixed + rotation * (used - fixed)) % max(1, count - fixed)
        return jnp.zeros((count,), jnp.int32).at[ranking[jnp.where(places < fixed, places, passed)]].set(jnp.asarray(lengths, jnp.int32))

    lengths = jnp.where(number % 4 == 0, named(crowded, number // 4), named(usual, number - number // 4 - 1))
    mixed = jax.random.permutation(jax.random.fold_in(own, 3), count)
    source_of, taker = mixed[0:count // 2 * 2:2], mixed[1:count // 2 * 2:2]
    margin = jnp.minimum(lengths[source_of] - 1, bound - lengths[taker]) // 2
    margin = jnp.where((source_of == ranking[0]) | (taker == ranking[0]) | (lengths[taker] == 0), 0, jnp.maximum(margin, 0))
    passed = jax.random.randint(jax.random.fold_in(own, 4), (count // 2,), 0, 1 << 20) % (margin + 1)
    lengths = lengths.at[source_of].add(-passed).at[taker].add(passed)
    items = jnp.searchsorted(jnp.cumsum(lengths), jnp.arange(rows * top), side="right").astype(jnp.int32)
    listing = items.reshape(top, rows).T
    listing = listing[jax.random.permutation(jax.random.fold_in(own, 1), rows)]
    rotation = jax.random.randint(jax.random.fold_in(own, 2), (rows, 1), 0, top)
    return jnp.take_along_axis(listing, (jnp.arange(top)[None, :] + rotation) % top, axis=1)


def load_shares(amount, total, most, slope, full):
    weights = [(1 << 20) // math.isqrt(grade ** slope) + 1 for grade in range(1, amount + 1)]
    largest = most if full else min(most, max(-(-total // amount), total * weights[0] // sum(weights)))
    least = 1 if total - largest >= amount - 1 else 0
    holding, spare = [largest] + [least] * (amount - 1), total - largest - least * (amount - 1)
    while spare > 0:
        candidates = [i for i in range(1, amount) if holding[i] < largest] or [i for i in range(1, amount) if holding[i] < most]
        pool, budget = sum([weights[i] for i in candidates]), spare
        for i in candidates:
            addition = min(most - holding[i], max(1, budget * weights[i] // pool), spare)
            holding[i] = holding[i] + addition
            spare = spare - addition
    return np.array(holding)


def noise(own_key, extent, spread, bound, pieces=(), kind=jnp.bfloat16):
    level = shard_levels(own_key, extent, pieces, -0.22, 0.18) if pieces else 1.0
    array = jax.random.normal(own_key, extent, jnp.float32) * spread * level
    return jnp.minimum(jnp.maximum(array, -bound), bound).astype(kind)


def setup_inputs(seed: int = 0) -> dict:
    arg_keys = jax.random.split(jax.random.key(seed), 7)
    interface = noise(arg_keys[0], (TOTAL, MODES), 1.0, 6.0, ((0, 256),))
    owners_keys = jax.random.split(jax.random.fold_in(arg_keys[1], 1), TOTAL // ROWS)
    owners_turns = jax.random.permutation(jax.random.fold_in(arg_keys[1], 3), TOTAL // ROWS)
    owners = jax.vmap(lambda own, number: assign_block(jax.random.fold_in(arg_keys[1], 2), own, number, ROWS, N_LEAF, 1, 2 * ROWS // N_LEAF, 2))(owners_keys, owners_turns).reshape((TOTAL, 1))
    keep_proj = noise(arg_keys[2], (LEVELS, MODES, MODES), MODES ** -0.5, 0.25)
    sibling_proj = noise(arg_keys[3], (LEVELS, MODES, MODES), MODES ** -0.5, 0.25)
    coupling = noise(arg_keys[4], (N_LEAF, MODES, MODES), MODES ** -0.5, 0.25, ((0, 64),))
    pattern = place_ends((jax.random.randint(arg_keys[5], (N_LEAF, NBLK, NBLK), 0, 2) < 1).astype(jnp.int32), jax.random.fold_in(arg_keys[5], 1), 0, 1)
    return dict(interface=interface, owners=owners, keep_proj=keep_proj, sibling_proj=sibling_proj, coupling=coupling, pattern=pattern)


epsilon = 1e-06

def expand_mask(mask_block):
    return jnp.repeat(jnp.repeat(mask_block, BS, axis=0), BS, axis=1)

def reference(interface, owners, keep_proj, sibling_proj, coupling, pattern):
    current = interface
    for tree_level in range(LEVELS):
        blocked = current.reshape(N_LEAF, N_BLK * ROWS, MODES)
        partner = np.arange(N_LEAF) ^ 1 << tree_level
        sibling = blocked[partner].reshape(-1, MODES)
        combined = jnp.dot(current, keep_proj[tree_level], preferred_element_type=jnp.float32)
        combined = combined + jnp.dot(sibling, sibling_proj[tree_level], preferred_element_type=jnp.float32)
        scale_rows = lax.rsqrt(lax.optimization_barrier(jnp.mean(combined * combined, axis=1, keepdims=True)) + epsilon)
        current = (combined * scale_rows).astype(jnp.bfloat16)
    capacity = 2 * ROWS // N_LEAF
    target = owners[:, 0].reshape(N_LEAF * N_BLK, ROWS).astype(jnp.int32)
    onehot = (target[:, :, None] == jnp.arange(N_LEAF, dtype=jnp.int32)[None, None, :]).astype(jnp.int32)
    slot_index = (lax.optimization_barrier(jnp.sum(jnp.cumsum(onehot, axis=1) * onehot, axis=2)) - 1).astype(jnp.int32)
    position = (target * capacity + slot_index).astype(jnp.int32)
    source = current.reshape(N_LEAF * N_BLK, ROWS, MODES)

    def fill_rows(rows_in, where):
        return jnp.zeros((N_LEAF * capacity, MODES), current.dtype).at[where].set(rows_in)
    outgoing = jax.vmap(fill_rows)(source, position)
    outgoing = outgoing.reshape(N_LEAF, N_BLK, N_LEAF, capacity, MODES).transpose(2, 1, 0, 3, 4)

    def apply_owner(operands):
        block_rows, weight, mask_block = operands
        dense = weight * expand_mask(mask_block).astype(weight.dtype)
        product = jnp.dot(block_rows.reshape(-1, MODES), dense, preferred_element_type=jnp.float32)
        return product.astype(jnp.bfloat16).reshape(block_rows.shape)
    coupled = lax.map(apply_owner, (outgoing, coupling, pattern))
    returned = coupled.transpose(2, 1, 0, 3, 4).reshape(N_LEAF * N_BLK, N_LEAF * capacity, MODES)
    result = jax.vmap(lambda rows_in, where: rows_in[where])(returned, position)
    return result.reshape(-1, MODES)
```

```python
import jax
import jax.numpy as jnp
from jax import lax
from jax.experimental import pallas as pl
from jax.experimental.pallas import tpu as pltpu
from jax.sharding import PartitionSpec as P

BS = 64
LEVELS = 3
EPS = 1e-06
CHUNKS = 8
PIECES = 2
F32, BF16, I32 = jnp.float32, jnp.bfloat16, jnp.int32


def leaf_of(y, x, zh, c):
    return ((lax.rem(y + 4, 4) * 4 + lax.rem(x + 4, 4)) * 2 + zh) * 2 + c


def kernel(x_ref, own_col, own_row, keep, sib, coup, pat, out_ref,
           twin, cur1, far, cur2, side, cur3, wall, packed, rbuf, res, ret, pmat, umat, acc,
           twin_s, twin_r, far_s, far_r, side_s, side_r, zc_s, zc_r, g_s, g_r, d_s, d_r, b_s, b_r):
    rows, modes = x_ref.shape
    size = rows // CHUNKS
    leaf, zl = lax.axis_index("leaf"), lax.axis_index("blk")
    c, zh = lax.rem(leaf, 2), lax.rem(leaf // 2, 2)
    x, y = lax.rem(leaf // 4, 4), leaf // 16
    z = zh * 4 + zl

    def at(dy=0, dx=0, core=None):
        return (leaf_of(y + dy, x + dx, zh, c if core is None else core), zl)

    def at_z(dz):
        t = lax.rem(z + dz + 8, 8)
        return (leaf_of(y, x, t // 4, c), lax.rem(t, 4))

    twin_dev = at(core=1 - c)
    far_dev = at_z(4)
    side_dev = at(dx=1 - 2 * lax.rem(x, 2))
    skip_dev = at(dy=2)
    knight_dev = at(dy=1, dx=2)
    unknight_dev = at(dy=-1, dx=2)
    around = [at(dx=1, core=s) for s in range(2)] + [at(dx=-1, core=s) for s in range(2)]
    around += [at(dy=1, core=s) for s in range(2)] + [at(dy=-1, core=s) for s in range(2)]
    peers = [twin_dev, far_dev, at_z(1), at_z(-1), skip_dev, knight_dev, unknight_dev] + around

    barrier = pltpu.get_barrier_semaphore()
    for peer in peers:
        pl.semaphore_signal(barrier, inc=1, device_id=peer, device_id_type=pl.DeviceIdType.MESH)
    pl.semaphore_wait(barrier, len(peers))

    sends = []

    def send(src, dst, ss, rs, dev):
        copy = pltpu.make_async_remote_copy(
            src_ref=src, dst_ref=dst, send_sem=ss, recv_sem=rs,
            device_id=dev, device_id_type=pl.DeviceIdType.MESH)
        copy.start()
        sends.append(copy)

    def arrived(dst, ss, rs, dev):
        pltpu.make_async_remote_copy(
            src_ref=dst, dst_ref=dst, send_sem=ss, recv_sem=rs,
            device_id=dev, device_id_type=pl.DeviceIdType.MESH).wait_recv()

    def part(i):
        return pl.ds(i * size, size)

    for i in range(CHUNKS):
        send(x_ref.at[part(i)], twin.at[part(i)], twin_s.at[i], twin_r.at[i], twin_dev)

    grid_r = lax.broadcasted_iota(I32, (modes, 8), 0) // BS
    grid_c = lax.broadcasted_iota(I32, (modes, 8), 1)
    spread = (grid_r == grid_c).astype(F32).astype(BF16)
    wide_r = lax.broadcasted_iota(I32, (8, modes), 0)
    wide_c = lax.broadcasted_iota(I32, (8, modes), 1) // BS
    spread_t = (wide_r == wide_c).astype(F32).astype(BF16)
    half = jnp.dot(spread, pat[0].astype(F32).astype(BF16), preferred_element_type=F32).astype(BF16)
    mask = jnp.dot(half, spread_t, preferred_element_type=F32).astype(BF16)
    mine, other = y * 2 + zh, y * 2 + (1 - zh)
    wall[mine] = coup[0] * mask

    up = 1 - 2 * c
    step = jnp.where(c == 0, zl, 3 - zl)
    next_dev, prev_dev = at_z(up), at_z(-up)
    deep = modes // PIECES
    chain_slot = jnp.where(step == 3, mine, other)

    def chain(p):
        piece = wall.at[chain_slot, pl.ds(p * deep, deep)]
        return pltpu.make_async_remote_copy(
            src_ref=piece, dst_ref=piece, send_sem=zc_s.at[p], recv_sem=zc_r.at[p],
            device_id=next_dev, device_id_type=pl.DeviceIdType.MESH)

    def chain_arrived(p):
        arrived(wall.at[other, pl.ds(p * deep, deep)], zc_s.at[p], zc_r.at[p], prev_dev)

    @pl.when(step == 3)
    def _():
        for p in range(PIECES):
            chain(p).start()

    def gather_send(slot, n, dev):
        send(wall.at[slot], wall.at[slot], g_s.at[n], g_r.at[n], dev)

    def gather_arrived(slot, n, dev):
        arrived(wall.at[slot], g_s.at[n], g_r.at[n], dev)

    y2, yn, yp = lax.rem(y + 2, 4), lax.rem(y + 3, 4), lax.rem(y + 1, 4)
    gather_send(mine, 0, skip_dev)
    gather_send(mine, 1, knight_dev)

    def level(l, mine_ref, other_ref, dst, i):
        total = jnp.dot(mine_ref[part(i)], keep[l], preferred_element_type=F32)
        total = total + jnp.dot(other_ref[part(i)], sib[l], preferred_element_type=F32)
        scale = lax.rsqrt(jnp.mean(total * total, axis=1, keepdims=True) + EPS)
        dst[part(i)] = (total * scale).astype(BF16)

    for i in range(CHUNKS):
        arrived(twin.at[part(i)], twin_s.at[i], twin_r.at[i], twin_dev)
        level(0, x_ref, twin, cur1, i)
        send(cur1.at[part(i)], far.at[part(i)], far_s.at[i], far_r.at[i], far_dev)

    colour = lax.rem(x + 2 * lax.rem(y, 2), 4)

    def base_of(o):
        oc, ozh, ox, oy = o & 1, (o >> 1) & 1, (o >> 2) & 3, o >> 4
        rel = (ox + 2 * (oy & 1) - colour + 4) & 3
        return ((((oy >> 1) * 4 + rel) * 2 + oc) * 4 + (oy & 1) * 2 + ozh) * 32

    tri_r = lax.broadcasted_iota(I32, (rows, rows), 0)
    tri_c = lax.broadcasted_iota(I32, (rows, rows), 1)
    pmat[0] = (tri_c < tri_r).astype(F32).astype(BF16)
    pmat[1] = (tri_r < tri_c).astype(F32).astype(BF16)
    hot = (own_col[...] == lax.broadcasted_iota(I32, (rows, 128), 1)).astype(F32)
    rank = jnp.sum(jnp.dot(pmat[0], hot.astype(BF16), preferred_element_type=F32) * hot, axis=1, keepdims=True)
    pos_col = base_of(own_col[...]) + rank.astype(I32)
    hot = (own_row[...] == lax.broadcasted_iota(I32, (128, rows), 0)).astype(F32)
    rank = jnp.sum(jnp.dot(hot.astype(BF16), pmat[1], preferred_element_type=F32) * hot, axis=0, keepdims=True)
    pos_row = base_of(own_row[...]) + rank.astype(I32)
    for h in range(2):
        pmat[h] = (tri_r + h * rows == pos_row).astype(F32).astype(BF16)
        umat[h] = (tri_c + h * rows == pos_col).astype(F32).astype(BF16)

    for p in range(PIECES):
        @pl.when(step < 3)
        def _():
            chain_arrived(p)
            chain(p).start()

    def level2(i):
        arrived(side.at[part(i)], side_s.at[i], side_r.at[i], side_dev)
        level(2, cur2, side, cur3, i)

    for i in range(CHUNKS):
        arrived(far.at[part(i)], far_s.at[i], far_r.at[i], far_dev)
        level(1, cur1, far, cur2, i)
        send(cur2.at[part(i)], side.at[part(i)], side_s.at[i], side_r.at[i], side_dev)
        if i:
            level2(i - 1)
        if i == 2:
            @pl.when(step == 3)
            def _():
                for p in range(PIECES):
                    chain_arrived(p)
            gather_send(other, 2, skip_dev)
            gather_send(other, 3, knight_dev)
        if i == 4:
            gather_arrived(yn * 2 + zh, 1, unknight_dev)
            gather_send(yn * 2 + zh, 4, skip_dev)
        if i == 6:
            gather_arrived(yn * 2 + (1 - zh), 3, unknight_dev)
            gather_send(yn * 2 + (1 - zh), 5, skip_dev)
    level2(CHUNKS - 1)

    def block(ref, h, rel, core):
        return ref.at[pl.ds(((h * 4 + rel) * 2 + core) * 128, 128)]

    def source(h, n):
        if n == 1:
            return twin_dev
        if n < 4:
            return at(dx=-1, core=n - 2)
        if n < 6:
            return at(dx=1, core=n - 4)
        return at(dy=-1 if h == 0 else 1, core=n - 6)

    for h in range(2):
        for rel in (1, 3, 2, 0):
            first = (h * 4 + rel) * 256
            packed[pl.ds(first, 256)] = jnp.dot(
                pmat[h, pl.ds(rel * 256, 256), :], cur3[...], preferred_element_type=F32).astype(BF16)
            if rel == 0:
                rbuf[h, 0] = packed[pl.ds(first + c * 128, 128)]
                send(block(packed, h, 0, 1 - c), rbuf.at[h, 1], d_s.at[h, 1], d_r.at[h, 1], twin_dev)
                continue
            place = {1: 2, 3: 4, 2: 6}[rel]
            for s in range(2):
                dev = {1: at(dx=1, core=s), 3: at(dx=-1, core=s), 2: at(dy=1 if h == 0 else -1, core=s)}[rel]
                send(block(packed, h, rel, s), rbuf.at[h, place + c], d_s.at[h, place + s], d_r.at[h, place + c], dev)

    gather_arrived(y2 * 2 + zh, 0, skip_dev)
    gather_arrived(y2 * 2 + (1 - zh), 2, skip_dev)
    gather_arrived(yp * 2 + zh, 4, skip_dev)
    gather_arrived(yp * 2 + (1 - zh), 5, skip_dev)

    for h in range(2):
        for n in range(1, 8):
            arrived(rbuf.at[h, n], d_s.at[h, n], d_r.at[h, n], source(h, n))
        for e in range(4):
            lines = pl.ds(e * 32, 32)
            product = jnp.dot(rbuf[h, :, lines, :].reshape(256, modes), wall[h * 4 + e], preferred_element_type=F32)
            res[h, :, lines, :] = product.astype(BF16).reshape(8, 32, modes)
        for n, rel in ((2, 1), (3, 1), (4, 3), (5, 3), (6, 2), (7, 2), (1, 0)):
            send(res.at[h, n], block(ret, h, rel, c), b_s.at[h, n],
                 b_r.at[h, 1 if rel == 0 else rel * 2 + c], source(h, n))
        ret[pl.ds(h * 1024 + c * 128, 128)] = res[h, 0]

    for h in range(2):
        arrived(block(ret, h, 0, 1 - c), b_s.at[h, 1], b_r.at[h, 1], twin_dev)
        for rel in (1, 3, 2):
            for s in range(2):
                dev = {1: at(dx=1, core=s), 3: at(dx=-1, core=s), 2: at(dy=1 if h == 0 else -1, core=s)}[rel]
                arrived(block(ret, h, rel, s), b_s.at[h, rel * 2 + s], b_r.at[h, rel * 2 + s], dev)
        got = jnp.dot(umat[h], ret[pl.ds(h * 1024, 1024)], preferred_element_type=F32)
        if h == 0:
            acc[...] = got
        else:
            out_ref[...] = (acc[...] + got).astype(BF16)

    for copy in sends:
        copy.wait_send()
    for p in range(PIECES):
        chain(p).wait_send()


def local(interface, owners, keep_proj, sibling_proj, coupling, pattern):
    rows, modes = interface.shape
    vmem = pl.BlockSpec(memory_space=pltpu.VMEM)
    dma = pltpu.SemaphoreType.DMA
    return pl.pallas_call(
        kernel,
        out_shape=jax.ShapeDtypeStruct((rows, modes), BF16),
        in_specs=[vmem] * 7,
        out_specs=vmem,
        scratch_shapes=[pltpu.VMEM((rows, modes), BF16)] * 6
        + [
            pltpu.VMEM((8, modes, modes), BF16),
            pltpu.VMEM((2 * rows, modes), BF16),
            pltpu.VMEM((2, 8, 128, modes), BF16),
            pltpu.VMEM((2, 8, 128, modes), BF16),
            pltpu.VMEM((2 * rows, modes), BF16),
            pltpu.VMEM((2, rows, rows), BF16),
            pltpu.VMEM((2, rows, rows), BF16),
            pltpu.VMEM((rows, modes), F32),
        ]
        + [dma((CHUNKS,))] * 6
        + [dma((PIECES,))] * 2
        + [dma((6,))] * 2
        + [dma((2, 8))] * 4,
        compiler_params=pltpu.CompilerParams(
            collective_id=0, has_side_effects=True, vmem_limit_bytes=60 << 20),
        name="condense",
    )(interface, owners, owners.reshape(1, rows), keep_proj, sibling_proj, coupling, pattern)


def solution(mesh):
    in_specs = (
        P(("leaf", "blk"), None),
        P(("leaf", "blk"), None),
        P(),
        P(),
        P("leaf", None, None),
        P("leaf", None, None),
    )
    out_specs = P(("leaf", "blk"), None)
    return jax.shard_map(local, mesh=mesh, in_specs=in_specs, out_specs=out_specs, check_vma=False)
```

```python
import jax
import jax.numpy as jnp
from jax import lax
from jax.experimental import pallas as pl
from jax.experimental.pallas import tpu as pltpu
from jax.sharding import PartitionSpec as P

BS = 64
LEVELS = 3
EPS = 1e-06
CHUNKS = 8
PIECES = 4
METER = False
F32, BF16, I32 = jnp.float32, jnp.bfloat16, jnp.int32


REACH = (
    ((0, 0), (0, 0)),
    ((2, 0), (0, 2)),
    ((1, 1), (-1, -1)),
    ((-1, 1), (1, -1)),
    ((1, 0), (1, 0)),
    ((-1, 0), (-1, 0)),
    ((0, 1), (0, 1)),
    ((0, -1), (0, -1)),
)


def leaf_of(y, x, zh, c):
    return ((lax.rem(y + 4, 4) * 4 + lax.rem(x + 4, 4)) * 2 + zh) * 2 + c


def kernel(x_ref, own_row, keep, sib, coup, pat, out_ref,
           twin, cur1, far, cur2, side, cur3, wall, packed, rbuf, res, ret, pmat, umat, acc, pos,
           twin_s, twin_r, far_s, far_r, side_s, side_r, zc_s, zc_r, g_s, g_r, d_s, d_r, b_s, b_r):
    rows, modes = x_ref.shape
    size = rows // CHUNKS
    leaf, zl = lax.axis_index("leaf"), lax.axis_index("blk")
    c, zh = lax.rem(leaf, 2), lax.rem(leaf // 2, 2)
    x, y = lax.rem(leaf // 4, 4), leaf // 16
    z = zh * 4 + zl

    def at(dx=0, dy=0, core=None):
        return (leaf_of(y + dy, x + dx, zh, c if core is None else core), zl)

    def at_z(dz):
        t = lax.rem(z + dz + 8, 8)
        return (leaf_of(y, x, t // 4, c), lax.rem(t, 4))

    twin_dev = at(core=1 - c)
    far_dev = at_z(4)
    side_dev = at(dx=1 - 2 * lax.rem(x, 2))
    pair_dev = at(2, 2)
    peers = [twin_dev, far_dev, at_z(1), at_z(-1), pair_dev]
    near = ((2, 0), (0, 2), (1, 1), (-1, -1), (-1, 1), (1, -1), (1, 0), (-1, 0), (0, 1), (0, -1))
    peers += [at(dx, dy, s) for dx, dy in near for s in range(2)]

    barrier = pltpu.get_barrier_semaphore()
    for peer in peers:
        pl.semaphore_signal(barrier, inc=1, device_id=peer, device_id_type=pl.DeviceIdType.MESH)
    pl.semaphore_wait(barrier, len(peers))

    sends = []

    def send(src, dst, ss, rs, dev):
        copy = pltpu.make_async_remote_copy(
            src_ref=src, dst_ref=dst, send_sem=ss, recv_sem=rs,
            device_id=dev, device_id_type=pl.DeviceIdType.MESH)
        copy.start()
        sends.append(copy)

    def arrived(dst, ss, rs, dev):
        pltpu.make_async_remote_copy(
            src_ref=dst, dst_ref=dst, send_sem=ss, recv_sem=rs,
            device_id=dev, device_id_type=pl.DeviceIdType.MESH).wait_recv()

    def part(i):
        return pl.ds(i * size, size)

    for i in range(CHUNKS):
        send(x_ref.at[part(i)], twin.at[part(i)], twin_s.at[i], twin_r.at[i], twin_dev)

    def level(l, mine_ref, other_ref, dst, i):
        total = jnp.dot(mine_ref[part(i)], keep[l], preferred_element_type=F32)
        total = total + jnp.dot(other_ref[part(i)], sib[l], preferred_element_type=F32)
        scale = lax.rsqrt(jnp.mean(total * total, axis=1, keepdims=True) + EPS)
        dst[part(i)] = (total * scale).astype(BF16)

    def far_send(i):
        send(cur1.at[part(i)], far.at[part(i)], far_s.at[i], far_r.at[i], far_dev)

    for i in range(CHUNKS):
        arrived(twin.at[part(i)], twin_s.at[i], twin_r.at[i], twin_dev)
        level(0, x_ref, twin, cur1, i)
        far_send(i)

    grid_r = lax.broadcasted_iota(I32, (modes, 8), 0) // BS
    grid_c = lax.broadcasted_iota(I32, (modes, 8), 1)
    spread = (grid_r == grid_c).astype(F32).astype(BF16)
    wide_r = lax.broadcasted_iota(I32, (8, modes), 0)
    wide_c = lax.broadcasted_iota(I32, (8, modes), 1) // BS
    spread_t = (wide_r == wide_c).astype(F32).astype(BF16)
    half = jnp.dot(spread, pat[0].astype(F32).astype(BF16), preferred_element_type=F32).astype(BF16)
    mask = jnp.dot(half, spread_t, preferred_element_type=F32).astype(BF16)
    upper = y // 2
    wall[upper] = coup[0] * mask
    send(wall.at[upper], wall.at[upper], g_s.at[0], g_r.at[0], pair_dev)

    up = 1 - 2 * c
    step = jnp.where(c == 0, zl, 3 - zl)
    next_dev, prev_dev = at_z(up), at_z(-up)
    deep = modes // PIECES

    def chain(n):
        col, p = n // PIECES, n % PIECES
        piece = pl.ds(p * deep, deep)
        return pltpu.make_async_remote_copy(
            src_ref=wall.at[jnp.where(step == 3, 0, 2) + col, piece], dst_ref=wall.at[2 + col, piece],
            send_sem=zc_s.at[n], recv_sem=zc_r.at[n],
            device_id=next_dev, device_id_type=pl.DeviceIdType.MESH)

    def chain_arrived(n):
        arrived(wall.at[2 + n // PIECES, pl.ds(n % PIECES * deep, deep)], zc_s.at[n], zc_r.at[n], prev_dev)

    def base_of(o):
        oc, ozh, ox, oy = o & 1, (o >> 1) & 1, (o >> 2) & 3, o >> 4
        dy = (oy - y + 4) & 3
        dx = (ox - x + 4 + (dy & 2)) & 3
        dy = dy & 1
        place = ((dx + dy) & 1) * 4 + dy * 2 + (dx >> 1)
        return ((((ozh ^ zh) * 8 + place) * 2 + oc) * 2 + (oy >> 1)) * 32

    tri_r = lax.broadcasted_iota(I32, (rows, rows), 0)
    tri_c = lax.broadcasted_iota(I32, (rows, rows), 1)

    def prepare(n):
        if n == 0:
            umat[0] = (tri_r < tri_c).astype(F32).astype(BF16)
            hot = (own_row[...] == lax.broadcasted_iota(I32, (64, rows), 0)).astype(F32)
            rank = jnp.sum(jnp.dot(hot.astype(BF16), umat[0], preferred_element_type=F32) * hot, axis=0, keepdims=True)
            pos[...] = base_of(own_row[...]) + rank.astype(I32)
        elif n < 3:
            pmat[n - 1] = (tri_r + (n - 1) * rows == pos[...]).astype(F32).astype(BF16)
        else:
            line = jnp.where(tri_r == tri_c, pos[...], 0)
            column = jnp.sum(line.astype(F32), axis=1, keepdims=True).astype(I32)
            umat[n - 3] = (tri_c + (n - 3) * rows == column).astype(F32).astype(BF16)

    def level2(i):
        arrived(side.at[part(i)], side_s.at[i], side_r.at[i], side_dev)
        level(2, cur2, side, cur3, i)

    def relay(col):
        @pl.when(step < 3)
        def _():
            for p in range(PIECES):
                chain_arrived(col * PIECES + p)
                chain(col * PIECES + p).start()

    for i in range(CHUNKS):
        arrived(far.at[part(i)], far_s.at[i], far_r.at[i], far_dev)
        if i == CHUNKS - 1:
            arrived(wall.at[1 - upper], g_s.at[0], g_r.at[0], pair_dev)

            @pl.when(step == 3)
            def _():
                for n in range(2 * PIECES):
                    chain(n).start()
        level(1, cur1, far, cur2, i)
        send(cur2.at[part(i)], side.at[part(i)], side_s.at[i], side_r.at[i], side_dev)
        if i:
            level2(i - 1)
        if i < 5:
            prepare(i)
    level2(CHUNKS - 1)

    def block(ref, g, q, core):
        return ref.at[pl.ds(((g * 8 + q) * 2 + core) * 64, 64)]

    def source(q, s):
        dx, dy = REACH[q][0]
        ex, ey = REACH[q][1]
        return at(jnp.where(c == 0, -dx, -ex), jnp.where(c == 0, -dy, -ey), s)

    def number(g, q, s):
        return (g * 8 + q) * 2 + s

    def rows_send(g, q):
        if q == 0:
            send(block(packed, g, 0, 1 - c), rbuf.at[g, 0, 0], d_s.at[g * 16], d_r.at[g * 16], twin_dev)
            return
        for s in range(2):
            send(block(packed, g, q, s), rbuf.at[g, q, c],
                 d_s.at[number(g, q, s)], d_r.at[number(g, q, c)], at(*REACH[q][s], s))

    def pack(g, k):
        packed[pl.ds(g * 1024 + k * 256, 256)] = jnp.dot(
            pmat[g, pl.ds(k * 256, 256), :], cur3[...], preferred_element_type=F32).astype(BF16)
        if k == 0:
            rbuf[g, 0, 1] = packed[pl.ds(g * 1024 + c * 64, 64)]

    def rows_arrived(g, q):
        if q == 0:
            arrived(rbuf.at[g, 0, 0], d_s.at[g * 16], d_r.at[g * 16], twin_dev)
            return
        for s in range(2):
            n = number(g, q, s)
            arrived(rbuf.at[g, q, s], d_s.at[n], d_r.at[n], source(q, s))

    def couple(g):
        for e in range(2):
            lines = pl.ds(e * 32, 32)
            left = rbuf[g, :, :, lines, :].reshape(512, modes)
            product = jnp.dot(left, wall[g * 2 + e], preferred_element_type=F32)
            res[g, :, :, lines, :] = product.astype(BF16).reshape(8, 2, 32, modes)

    def result_send(g, q):
        if q == 0:
            send(res.at[g, 0, 0], block(ret, g, 0, c), b_s.at[g * 16], b_r.at[g * 16], twin_dev)
            ret[pl.ds(g * 1024 + c * 64, 64)] = res[g, 0, 1]
            return
        for s in range(2):
            send(res.at[g, q, s], block(ret, g, q, c), b_s.at[number(g, q, s)], b_r.at[number(g, q, c)], source(q, s))

    def result_arrived(g, q):
        if q == 0:
            arrived(block(ret, g, 0, 1 - c), b_s.at[g * 16], b_r.at[g * 16], twin_dev)
            return
        for s in range(2):
            n = number(g, q, s)
            arrived(block(ret, g, q, s), b_s.at[n], b_r.at[n], at(*REACH[q][s], s))

    for g in range(2):
        for k in range(4):
            pack(g, k)
            if g == 0 or not METER:
                for q in (2 * k + 1, 2 * k):
                    rows_send(g, q)
        relay(g)
    for q in range(8):
        rows_arrived(0, q)
    if METER:
        for q in (1, 2, 3, 4, 5, 6, 7, 0):
            rows_send(1, q)
    couple(0)
    for q in (1, 2, 3, 4, 5, 6, 7, 0):
        result_send(0, q)

    @pl.when(step == 3)
    def _():
        for n in range(2 * PIECES):
            chain_arrived(n)
    for q in range(8):
        rows_arrived(1, q)
    couple(1)
    for q in (1, 2, 3, 4, 5, 6, 7, 0):
        result_send(1, q)
    for q in range(8):
        result_arrived(0, q)
    acc[...] = jnp.dot(umat[0], ret[pl.ds(0, 1024)], preferred_element_type=F32)
    for q in range(8):
        result_arrived(1, q)
    got = jnp.dot(umat[1], ret[pl.ds(1024, 1024)], preferred_element_type=F32)
    out_ref[...] = (acc[...] + got).astype(BF16)

    for copy in sends:
        copy.wait_send()
    for n in range(2 * PIECES):
        chain(n).wait_send()


def local(interface, owners, keep_proj, sibling_proj, coupling, pattern):
    rows, modes = interface.shape
    vmem = pl.BlockSpec(memory_space=pltpu.VMEM)
    dma = pltpu.SemaphoreType.DMA
    return pl.pallas_call(
        kernel,
        out_shape=jax.ShapeDtypeStruct((rows, modes), BF16),
        in_specs=[vmem] * 6,
        out_specs=vmem,
        scratch_shapes=[pltpu.VMEM((rows, modes), BF16)] * 6
        + [
            pltpu.VMEM((4, modes, modes), BF16),
            pltpu.VMEM((2 * rows, modes), BF16),
            pltpu.VMEM((2, 8, 2, 64, modes), BF16),
            pltpu.VMEM((2, 8, 2, 64, modes), BF16),
            pltpu.VMEM((2 * rows, modes), BF16),
            pltpu.VMEM((2, rows, rows), BF16),
            pltpu.VMEM((2, rows, rows), BF16),
            pltpu.VMEM((rows, modes), F32),
            pltpu.VMEM((1, rows), I32),
        ]
        + [dma((CHUNKS,))] * 6
        + [dma((2 * PIECES,))] * 2
        + [dma((1,))] * 2
        + [dma((32,))] * 4,
        compiler_params=pltpu.CompilerParams(
            collective_id=0, has_side_effects=True, vmem_limit_bytes=60 << 20),
        name="condense",
    )(interface, owners.reshape(1, rows), keep_proj, sibling_proj, coupling, pattern)


def solution(mesh):
    in_specs = (
        P(("leaf", "blk"), None),
        P(("leaf", "blk"), None),
        P(),
        P(),
        P("leaf", None, None),
        P("leaf", None, None),
    )
    out_specs = P(("leaf", "blk"), None)
    return jax.shard_map(local, mesh=mesh, in_specs=in_specs, out_specs=out_specs, check_vma=False)
```

```python
import jax
import jax.numpy as jnp
from jax import lax
from jax.experimental import pallas as pl
from jax.experimental.pallas import tpu as pltpu
from jax.sharding import PartitionSpec as P

BS = 64
LEVELS = 3
EPS = 1e-06
SIZES = (128, 128, 128, 128, 128, 128, 128, 64, 64)
CHUNKS = len(SIZES)
PIECES = 4
F32, BF16, I32 = jnp.float32, jnp.bfloat16, jnp.int32


REACH = (
    ((0, 0), (0, 0)),
    ((2, 0), (0, 2)),
    ((1, 1), (-1, -1)),
    ((-1, 1), (1, -1)),
    ((1, 0), (1, 0)),
    ((-1, 0), (-1, 0)),
    ((0, 1), (0, 1)),
    ((0, -1), (0, -1)),
)


def leaf_of(y, x, zh, c):
    return ((lax.rem(y + 4, 4) * 4 + lax.rem(x + 4, 4)) * 2 + zh) * 2 + c


def kernel(x_hbm, own_hbm, keep_hbm, sib_hbm, coup_hbm, pat_hbm, out_ref,
           x_ref, own_row, keep, sib, coup, pat, load_s, twin, cur1, far, cur2, side, cur3, wall, packed, rbuf, res, ret, pmat, umat, acc, pos,
           twin_s, twin_r, far_s, far_r, side_s, side_r, zc_s, zc_r, g_s, g_r, d_s, d_r, b_s, b_r):
    rows, modes = x_hbm.shape
    leaf, zl = lax.axis_index("leaf"), lax.axis_index("blk")
    c, zh = lax.rem(leaf, 2), lax.rem(leaf // 2, 2)
    x, y = lax.rem(leaf // 4, 4), leaf // 16
    z = zh * 4 + zl

    def at(dx=0, dy=0, core=None):
        return (leaf_of(y + dy, x + dx, zh, c if core is None else core), zl)

    def at_z(dz):
        t = lax.rem(z + dz + 8, 8)
        return (leaf_of(y, x, t // 4, c), lax.rem(t, 4))

    twin_dev = at(core=1 - c)
    far_dev = at_z(4)
    side_dev = at(dx=1 - 2 * lax.rem(x, 2))
    pair_dev = at(2, 2)
    peers = [twin_dev, far_dev, at_z(1), at_z(-1), pair_dev]
    near = ((2, 0), (0, 2), (1, 1), (-1, -1), (-1, 1), (1, -1), (1, 0), (-1, 0), (0, 1), (0, -1))
    peers += [at(dx, dy, s) for dx, dy in near for s in range(2)]

    barrier = pltpu.get_barrier_semaphore()
    for peer in peers:
        pl.semaphore_signal(barrier, inc=1, device_id=peer, device_id_type=pl.DeviceIdType.MESH)

    loads = {}

    def load(name, src, dst):
        loads[name] = pltpu.make_async_copy(src, dst, load_s.at[len(loads)])
        loads[name].start()

    load("x", x_hbm, x_ref)
    load("keep0", keep_hbm.at[0], keep.at[0])
    load("sib0", sib_hbm.at[0], sib.at[0])
    load("coup", coup_hbm, coup)
    load("pat", pat_hbm, pat)
    load("own", own_hbm, own_row)
    for l in (1, 2):
        load(f"keep{l}", keep_hbm.at[l], keep.at[l])
        load(f"sib{l}", sib_hbm.at[l], sib.at[l])
    pl.semaphore_wait(barrier, len(peers))

    sends = []

    def send(src, dst, ss, rs, dev):
        copy = pltpu.make_async_remote_copy(
            src_ref=src, dst_ref=dst, send_sem=ss, recv_sem=rs,
            device_id=dev, device_id_type=pl.DeviceIdType.MESH)
        copy.start()
        sends.append(copy)

    def arrived(dst, ss, rs, dev):
        pltpu.make_async_remote_copy(
            src_ref=dst, dst_ref=dst, send_sem=ss, recv_sem=rs,
            device_id=dev, device_id_type=pl.DeviceIdType.MESH).wait_recv()

    def part(i):
        return pl.ds(sum(SIZES[:i]), SIZES[i])

    for i in range(CHUNKS):
        send(x_hbm.at[part(i)], twin.at[part(i)], twin_s.at[i], twin_r.at[i], twin_dev)

    def level(l, mine_ref, other_ref, dst, i):
        total = jnp.dot(mine_ref[part(i)], keep[l], preferred_element_type=F32)
        total = total + jnp.dot(other_ref[part(i)], sib[l], preferred_element_type=F32)
        scale = lax.rsqrt(jnp.mean(total * total, axis=1, keepdims=True) + EPS)
        dst[part(i)] = (total * scale).astype(BF16)

    def far_send(i):
        send(cur1.at[part(i)], far.at[part(i)], far_s.at[i], far_r.at[i], far_dev)

    for name in ("x", "keep0", "sib0"):
        loads[name].wait()
    for i in range(CHUNKS):
        arrived(twin.at[part(i)], twin_s.at[i], twin_r.at[i], twin_dev)
        level(0, x_ref, twin, cur1, i)
        far_send(i)

    loads["coup"].wait()
    loads["pat"].wait()
    grid_r = lax.broadcasted_iota(I32, (modes, 8), 0) // BS
    grid_c = lax.broadcasted_iota(I32, (modes, 8), 1)
    spread = (grid_r == grid_c).astype(F32).astype(BF16)
    wide_r = lax.broadcasted_iota(I32, (8, modes), 0)
    wide_c = lax.broadcasted_iota(I32, (8, modes), 1) // BS
    spread_t = (wide_r == wide_c).astype(F32).astype(BF16)
    half = jnp.dot(spread, pat[0].astype(F32).astype(BF16), preferred_element_type=F32).astype(BF16)
    mask = jnp.dot(half, spread_t, preferred_element_type=F32).astype(BF16)
    upper = y // 2
    wall[upper] = coup[0] * mask
    send(wall.at[upper], wall.at[upper], g_s.at[0], g_r.at[0], pair_dev)

    up = 1 - 2 * c
    step = jnp.where(c == 0, zl, 3 - zl)
    next_dev, prev_dev = at_z(up), at_z(-up)
    deep = modes // PIECES

    def chain(n):
        col, p = n // PIECES, n % PIECES
        piece = pl.ds(p * deep, deep)
        return pltpu.make_async_remote_copy(
            src_ref=wall.at[jnp.where(step == 3, 0, 2) + col, piece], dst_ref=wall.at[2 + col, piece],
            send_sem=zc_s.at[n], recv_sem=zc_r.at[n],
            device_id=next_dev, device_id_type=pl.DeviceIdType.MESH)

    def chain_arrived(n):
        arrived(wall.at[2 + n // PIECES, pl.ds(n % PIECES * deep, deep)], zc_s.at[n], zc_r.at[n], prev_dev)

    def base_of(o):
        oc, ozh, ox, oy = o & 1, (o >> 1) & 1, (o >> 2) & 3, o >> 4
        dy = (oy - y + 4) & 3
        dx = (ox - x + 4 + (dy & 2)) & 3
        dy = dy & 1
        place = ((dx + dy) & 1) * 4 + dy * 2 + (dx >> 1)
        return ((((ozh ^ zh) * 8 + place) * 2 + oc) * 2 + (oy >> 1)) * 32

    tri_r = lax.broadcasted_iota(I32, (rows, rows), 0)
    tri_c = lax.broadcasted_iota(I32, (rows, rows), 1)

    def prepare(n):
        if n == 0:
            umat[0] = (tri_r < tri_c).astype(F32).astype(BF16)
            hot = (own_row[...] == lax.broadcasted_iota(I32, (64, rows), 0)).astype(F32)
            rank = jnp.sum(jnp.dot(hot.astype(BF16), umat[0], preferred_element_type=F32) * hot, axis=0, keepdims=True)
            pos[...] = base_of(own_row[...]) + rank.astype(I32)
        elif n < 3:
            pmat[n - 1] = (tri_r + (n - 1) * rows == pos[...]).astype(F32).astype(BF16)
        else:
            line = jnp.where(tri_r == tri_c, pos[...], 0)
            column = jnp.sum(line.astype(F32), axis=1, keepdims=True).astype(I32)
            umat[n - 3] = (tri_c + (n - 3) * rows == column).astype(F32).astype(BF16)

    for name in ("own", "keep1", "sib1", "keep2", "sib2"):
        loads[name].wait()

    def level2(i):
        arrived(side.at[part(i)], side_s.at[i], side_r.at[i], side_dev)
        level(2, cur2, side, cur3, i)

    def relay(col):
        @pl.when(step < 3)
        def _():
            for p in range(PIECES):
                chain_arrived(col * PIECES + p)
                chain(col * PIECES + p).start()

    for i in range(CHUNKS):
        arrived(far.at[part(i)], far_s.at[i], far_r.at[i], far_dev)
        if i == CHUNKS - 1:
            arrived(wall.at[1 - upper], g_s.at[0], g_r.at[0], pair_dev)

            @pl.when(step == 3)
            def _():
                for n in range(2 * PIECES):
                    chain(n).start()
        level(1, cur1, far, cur2, i)
        send(cur2.at[part(i)], side.at[part(i)], side_s.at[i], side_r.at[i], side_dev)
        if i:
            level2(i - 1)
        if i < 5:
            prepare(i)
    level2(CHUNKS - 1)

    def block(ref, g, q, core):
        return ref.at[pl.ds(((g * 8 + q) * 2 + core) * 64, 64)]

    def source(q, s):
        dx, dy = REACH[q][0]
        ex, ey = REACH[q][1]
        return at(jnp.where(c == 0, -dx, -ex), jnp.where(c == 0, -dy, -ey), s)

    def number(g, q, s):
        return (g * 8 + q) * 2 + s

    def rows_send(g, q):
        if q == 0:
            send(block(packed, g, 0, 1 - c), rbuf.at[g, 0, 0], d_s.at[g * 16], d_r.at[g * 16], twin_dev)
            return
        for s in range(2):
            send(block(packed, g, q, s), rbuf.at[g, q, c],
                 d_s.at[number(g, q, s)], d_r.at[number(g, q, c)], at(*REACH[q][s], s))

    def pack(g, k):
        packed[pl.ds(g * 1024 + k * 256, 256)] = jnp.dot(
            pmat[g, pl.ds(k * 256, 256), :], cur3[...], preferred_element_type=F32).astype(BF16)
        if k == 0:
            rbuf[g, 0, 1] = packed[pl.ds(g * 1024 + c * 64, 64)]

    def rows_arrived(g, q):
        if q == 0:
            arrived(rbuf.at[g, 0, 0], d_s.at[g * 16], d_r.at[g * 16], twin_dev)
            return
        for s in range(2):
            n = number(g, q, s)
            arrived(rbuf.at[g, q, s], d_s.at[n], d_r.at[n], source(q, s))

    def couple(g):
        for e in range(2):
            lines = pl.ds(e * 32, 32)
            left = rbuf[g, :, :, lines, :].reshape(512, modes)
            product = jnp.dot(left, wall[g * 2 + e], preferred_element_type=F32)
            res[g, :, :, lines, :] = product.astype(BF16).reshape(8, 2, 32, modes)

    def result_send(g, q):
        if q == 0:
            send(res.at[g, 0, 0], block(ret, g, 0, c), b_s.at[g * 16], b_r.at[g * 16], twin_dev)
            ret[pl.ds(g * 1024 + c * 64, 64)] = res[g, 0, 1]
            return
        for s in range(2):
            send(res.at[g, q, s], block(ret, g, q, c), b_s.at[number(g, q, s)], b_r.at[number(g, q, c)], source(q, s))

    def result_arrived(g, q):
        if q == 0:
            arrived(block(ret, g, 0, 1 - c), b_s.at[g * 16], b_r.at[g * 16], twin_dev)
            return
        for s in range(2):
            n = number(g, q, s)
            arrived(block(ret, g, q, s), b_s.at[n], b_r.at[n], at(*REACH[q][s], s))

    for g in range(2):
        for k in range(4):
            pack(g, k)
            for q in (2 * k + 1, 2 * k):
                rows_send(g, q)
        relay(g)
    for q in range(8):
        rows_arrived(0, q)
    couple(0)
    for q in (1, 2, 3, 4, 5, 6, 7, 0):
        result_send(0, q)

    @pl.when(step == 3)
    def _():
        for n in range(2 * PIECES):
            chain_arrived(n)
    for q in range(8):
        rows_arrived(1, q)
    couple(1)
    for q in (1, 2, 3, 4, 5, 6, 7, 0):
        result_send(1, q)
    for q in range(8):
        result_arrived(0, q)
    acc[...] = jnp.dot(umat[0], ret[pl.ds(0, 1024)], preferred_element_type=F32)
    for q in range(4, 8):
        result_arrived(1, q)
    acc[...] += jnp.dot(umat[1, :, 512:], ret[pl.ds(1536, 512)], preferred_element_type=F32)
    for q in range(4):
        result_arrived(1, q)
    got = jnp.dot(umat[1, :, :512], ret[pl.ds(1024, 512)], preferred_element_type=F32)
    out_ref[...] = (acc[...] + got).astype(BF16)

    for copy in sends:
        copy.wait_send()
    for n in range(2 * PIECES):
        chain(n).wait_send()


def local(interface, owners, keep_proj, sibling_proj, coupling, pattern):
    rows, modes = interface.shape
    vmem = pl.BlockSpec(memory_space=pltpu.VMEM)
    dma = pltpu.SemaphoreType.DMA
    return pl.pallas_call(
        kernel,
        out_shape=pltpu.VMEM((rows, modes), BF16),
        in_specs=[pl.BlockSpec(memory_space=pltpu.HBM)] * 6,
        out_specs=vmem,
        scratch_shapes=[
            pltpu.VMEM((rows, modes), BF16),
            pltpu.VMEM((1, rows), I32),
            pltpu.VMEM(keep_proj.shape, BF16),
            pltpu.VMEM(sibling_proj.shape, BF16),
            pltpu.VMEM(coupling.shape, BF16),
            pltpu.VMEM(pattern.shape, I32),
            dma((10,)),
        ]
        + [pltpu.VMEM((rows, modes), BF16)] * 6
        + [
            pltpu.VMEM((4, modes, modes), BF16),
            pltpu.VMEM((2 * rows, modes), BF16),
            pltpu.VMEM((2, 8, 2, 64, modes), BF16),
            pltpu.VMEM((2, 8, 2, 64, modes), BF16),
            pltpu.VMEM((2 * rows, modes), BF16),
            pltpu.VMEM((2, rows, rows), BF16),
            pltpu.VMEM((2, rows, rows), BF16),
            pltpu.VMEM((rows, modes), F32),
            pltpu.VMEM((1, rows), I32),
        ]
        + [dma((CHUNKS,))] * 6
        + [dma((2 * PIECES,))] * 2
        + [dma((1,))] * 2
        + [dma((32,))] * 4,
        compiler_params=pltpu.CompilerParams(
            collective_id=0, has_side_effects=True, vmem_limit_bytes=56 << 20),
        name="condense",
    )(interface, owners.reshape(1, rows), keep_proj, sibling_proj, coupling, pattern)


def solution(mesh):
    in_specs = (
        P(("leaf", "blk"), None),
        P(("leaf", "blk"), None),
        P(),
        P(),
        P("leaf", None, None),
        P("leaf", None, None),
    )
    out_specs = P(("leaf", "blk"), None)
    return jax.shard_map(local, mesh=mesh, in_specs=in_specs, out_specs=out_specs, check_vma=False)
```

```python
import jax
import jax.numpy as jnp
from jax import lax
from jax.experimental import pallas as pl
from jax.experimental.pallas import tpu as pltpu
from jax.sharding import PartitionSpec as P

BS = 64
LEVELS = 3
EPS = 1e-06
SIZES = (128, 128, 128, 128, 128, 128, 128, 64, 64)
CHUNKS = len(SIZES)
PIECES = 4
RELAY = (
    ((0, 1), (), ()),
    ((2, 3), (0, 1), ()),
    ((4, 5), (2, 3), (0, 1)),
    ((6, 7), (4, 5), (2, 3)),
    ((), (6, 7), (4, 5)),
    ((), (), (6, 7)),
)
F32, BF16, I32 = jnp.float32, jnp.bfloat16, jnp.int32


REACH = (
    ((0, 0), (0, 0)),
    ((2, 0), (0, 2)),
    ((1, 1), (-1, -1)),
    ((1, -1), (-1, 1)),
    ((1, 0), (1, 0)),
    ((-1, 0), (-1, 0)),
    ((0, 1), (0, 1)),
    ((0, -1), (0, -1)),
)
SHARED = (
    (1, 2, 0), (1, 3, 0), (1, 1, 0), (1, 4, 0), (1, 4, 1), (0, 0, 0), (0, 0, 1),
    (2, 2, 1), (2, 3, 1), (2, 5, 0), (2, 5, 1), (3, 6, 0), (3, 6, 1),
)
BLOCKS = (
    SHARED + ((3, 1, 1), (4, 7, 0), (4, 7, 1)),
    SHARED + ((4, 7, 0), (4, 7, 1), (4, 1, 1)),
)


def leaf_of(y, x, zh, c):
    return ((lax.rem(y + 4, 4) * 4 + lax.rem(x + 4, 4)) * 2 + zh) * 2 + c


def kernel(x_hbm, own_hbm, keep_hbm, sib_hbm, coup_hbm, pat_hbm, out_ref,
           x_ref, own_all, keep, sib, coup, pat, load_s, cur3x, wide, twin, cur1, far, cur2, side, cur3, wall, packed, rbuf, res, ret, pmat, umat, acc, pos, own_s, own_r, cast_s, cast_r,
           twin_s, twin_r, far_s, far_r, side_s, side_r, zc_s, zc_r, g_s, g_r, d_s, d_r, b_s, b_r):
    rows, modes = x_hbm.shape
    leaf, zl = lax.axis_index("leaf"), lax.axis_index("blk")
    c, zh = lax.rem(leaf, 2), lax.rem(leaf // 2, 2)
    x, y = lax.rem(leaf // 4, 4), leaf // 16
    z = zh * 4 + zl

    def at(dx=0, dy=0, core=None):
        return (leaf_of(y + dy, x + dx, zh, c if core is None else core), zl)

    def at_z(dz):
        t = lax.rem(z + dz + 8, 8)
        return (leaf_of(y, x, t // 4, c), lax.rem(t, 4))

    twin_dev = at(core=1 - c)
    far_dev = at_z(4)
    hot = 1 - 2 * lax.rem(x, 2)
    side_dev = at(dx=hot)
    beside = (side_dev, at(dx=-hot), at(dy=-1), at(dy=1))
    pair_dev = at(2, 2)
    peers = [twin_dev, far_dev, at_z(1), at_z(-1), pair_dev]
    near = ((2, 0), (0, 2), (1, 1), (-1, -1), (-1, 1), (1, -1), (1, 0), (-1, 0), (0, 1), (0, -1))
    peers += [at(dx, dy, s) for dx, dy in near for s in range(2)]

    barrier = pltpu.get_barrier_semaphore()
    for peer in peers:
        pl.semaphore_signal(barrier, inc=1, device_id=peer, device_id_type=pl.DeviceIdType.MESH)

    loads = {}

    def load(name, src, dst):
        loads[name] = pltpu.make_async_copy(src, dst, load_s.at[len(loads)])
        loads[name].start()

    load("x", x_hbm, x_ref)
    load("keep0", keep_hbm.at[0], keep.at[0])
    load("sib0", sib_hbm.at[0], sib.at[0])
    load("coup", coup_hbm, coup)
    load("pat", pat_hbm, pat)
    load("own", own_hbm, own_all.at[0])
    for l in (1, 2):
        load(f"keep{l}", keep_hbm.at[l], keep.at[l])
        load(f"sib{l}", sib_hbm.at[l], sib.at[l])
    pl.semaphore_wait(barrier, len(peers))

    sends = []

    def send(src, dst, ss, rs, dev):
        copy = pltpu.make_async_remote_copy(
            src_ref=src, dst_ref=dst, send_sem=ss, recv_sem=rs,
            device_id=dev, device_id_type=pl.DeviceIdType.MESH)
        copy.start()
        sends.append(copy)

    def arrived(dst, ss, rs, dev):
        pltpu.make_async_remote_copy(
            src_ref=dst, dst_ref=dst, send_sem=ss, recv_sem=rs,
            device_id=dev, device_id_type=pl.DeviceIdType.MESH).wait_recv()

    def part(i):
        return pl.ds(sum(SIZES[:i]), SIZES[i])

    for i in range(CHUNKS):
        send(x_hbm.at[part(i)], twin.at[part(i)], twin_s.at[i], twin_r.at[i], twin_dev)

    def level(l, mine_ref, other_ref, dst, i):
        total = jnp.dot(mine_ref[part(i)], keep[l], preferred_element_type=F32)
        total = total + jnp.dot(other_ref[part(i)], sib[l], preferred_element_type=F32)
        scale = lax.rsqrt(jnp.mean(total * total, axis=1, keepdims=True) + EPS)
        dst[part(i)] = (total * scale).astype(BF16)

    def far_send(i):
        send(cur1.at[part(i)], far.at[part(i)], far_s.at[i], far_r.at[i], far_dev)

    for name in ("x", "keep0", "sib0", "own"):
        loads[name].wait()
    for n, slot in enumerate((1, 2, 4, 3)):
        send(own_all.at[0], own_all.at[slot], own_s.at[n], own_r.at[slot - 1], beside[n])
    for i in range(CHUNKS):
        arrived(twin.at[part(i)], twin_s.at[i], twin_r.at[i], twin_dev)
        level(0, x_ref, twin, cur1, i)
        far_send(i)

    loads["coup"].wait()
    loads["pat"].wait()
    grid_r = lax.broadcasted_iota(I32, (modes, 8), 0) // BS
    grid_c = lax.broadcasted_iota(I32, (modes, 8), 1)
    spread = (grid_r == grid_c).astype(F32).astype(BF16)
    wide_r = lax.broadcasted_iota(I32, (8, modes), 0)
    wide_c = lax.broadcasted_iota(I32, (8, modes), 1) // BS
    spread_t = (wide_r == wide_c).astype(F32).astype(BF16)
    half = jnp.dot(spread, pat[0].astype(F32).astype(BF16), preferred_element_type=F32).astype(BF16)
    mask = jnp.dot(half, spread_t, preferred_element_type=F32).astype(BF16)
    upper = y // 2
    wall[upper] = coup[0] * mask
    send(wall.at[upper], wall.at[upper], g_s.at[0], g_r.at[0], pair_dev)

    up = 1 - 2 * c
    step = jnp.where(c == 0, zl, 3 - zl)
    next_dev, prev_dev = at_z(up), at_z(-up)
    deep = modes // PIECES

    def chain(n):
        col, p = n // PIECES, n % PIECES
        piece = pl.ds(p * deep, deep)
        return pltpu.make_async_remote_copy(
            src_ref=wall.at[jnp.where(step == 3, 0, 2) + col, piece], dst_ref=wall.at[2 + col, piece],
            send_sem=zc_s.at[n], recv_sem=zc_r.at[n],
            device_id=next_dev, device_id_type=pl.DeviceIdType.MESH)

    def chain_arrived(n):
        arrived(wall.at[2 + n // PIECES, pl.ds(n % PIECES * deep, deep)], zc_s.at[n], zc_r.at[n], prev_dev)

    def base_of(o, home_x, home_y, towards):
        oc, ozh, ox, oy = o & 1, (o >> 1) & 1, (o >> 2) & 3, o >> 4
        dy = (oy - home_y) & 3
        dx = (towards * (ox - home_x) + (dy & 2)) & 3
        dy = dy & 1
        q = ((dx + dy) & 1) * 4 + dy * 2 + (dx >> 1)
        return ((((ozh ^ zh) * 8 + q) * 2 + oc) * 2 + (oy >> 1)) * 32

    homes = ((x, y, hot), (x + hot, y, -hot), (x - hot, y, -hot), (x, y - 1, hot), (x, y + 1, hot))
    tri_r = lax.broadcasted_iota(I32, (rows, rows), 0)
    tri_c = lax.broadcasted_iota(I32, (rows, rows), 1)

    def prepare(n):
        if n == 0:
            umat[0] = (tri_r < tri_c).astype(F32).astype(BF16)
            for k in range(5):
                if k:
                    arrived(own_all.at[k], own_s.at[k - 1], own_r.at[k - 1], beside[k - 1])
                mine = own_all[k]
                named = (mine == lax.broadcasted_iota(I32, (64, rows), 0)).astype(F32)
                rank = jnp.dot(named.astype(BF16), umat[0], preferred_element_type=F32)
                rank = jnp.sum(rank * named, axis=0, keepdims=True)
                pos[k] = base_of(mine, *homes[k]) + rank.astype(I32)
        elif n < 3:
            g = n - 1
            line = lax.broadcasted_iota(I32, (64, rows), 0)
            for j, (k, q, core) in enumerate(BLOCKS[g]):
                first = ((g * 8 + q) * 2 + core) * 64
                pmat[g, pl.ds(j * 64, 64), :] = (line + first == pos[k]).astype(F32).astype(BF16)
        else:
            line = jnp.where(tri_r == tri_c, pos[0], 0)
            column = jnp.sum(line.astype(F32), axis=1, keepdims=True).astype(I32)
            umat[n - 3] = (tri_c + (n - 3) * rows == column).astype(F32).astype(BF16)

    for name in ("keep1", "sib1", "keep2", "sib2"):
        loads[name].wait()

    def level2(i):
        arrived(side.at[part(i)], side_s.at[i], side_r.at[i], side_dev)
        level(2, cur2, side, cur3, i)
        for n, slot in enumerate((0, 2, 1)):
            send(cur3.at[part(i)], wide.at[slot, part(i)], cast_s.at[n, i], cast_r.at[slot, i], beside[n + 1])
        level(2, side, cur2, cur3x, i)

    def hand_on(pieces):
        for n in pieces:
            chain_arrived(n)
            chain(n).start()

    def relay(point):
        for place, pieces in enumerate(RELAY[point]):
            if pieces:
                pl.when(step == place)(lambda pieces=pieces: hand_on(pieces))

    for i in range(CHUNKS):
        arrived(far.at[part(i)], far_s.at[i], far_r.at[i], far_dev)
        if i == CHUNKS - 1:
            arrived(wall.at[1 - upper], g_s.at[0], g_r.at[0], pair_dev)

            @pl.when(step == 3)
            def _():
                for n in range(2 * PIECES):
                    chain(n).start()
        level(1, cur1, far, cur2, i)
        send(cur2.at[part(i)], side.at[part(i)], side_s.at[i], side_r.at[i], side_dev)
        if i:
            level2(i - 1)
        if i < 5:
            prepare(i)
    level2(CHUNKS - 1)
    relay(0)

    def block(ref, g, q, core):
        return ref.at[pl.ds(((g * 8 + q) * 2 + core) * 64, 64)]

    def reach(q, s):
        dx, dy = REACH[q][s]
        return at(dx * hot, dy, s)

    def source(q, s):
        (dx, dy), (ex, ey) = REACH[q]
        return at(jnp.where(c == 0, dx, ex) * hot, jnp.where(c == 0, -dy, -ey), s)

    def number(g, q, s):
        return (g * 8 + q) * 2 + s

    forward = {
        (1, 2, 0): at(0, 1, 0), (1, 3, 0): at(0, -1, 0), (1, 1, 0): at(-hot, 0, 0),
        (2, 2, 1): at(0, -1, 1), (2, 3, 1): at(0, 1, 1), (3, 1, 1): at(0, 1, 1), (4, 1, 1): at(0, -1, 1),
    }

    def pack(g, k):
        places = [j for j, entry in enumerate(BLOCKS[g]) if entry[0] == k]
        rows_of = cur3 if k == 0 else cur3x if k == 1 else wide.at[k - 2]
        span = pl.ds(places[0] * 64, len(places) * 64)
        base = g * 1024
        packed[pl.ds(base + places[0] * 64, len(places) * 64)] = jnp.dot(
            pmat[g, span, :], rows_of[...], preferred_element_type=F32).astype(BF16)
        for j in places:
            entry = BLOCKS[g][j]
            n = number(g, entry[1], c)
            if entry in forward:
                send(packed.at[pl.ds(base + j * 64, 64)], rbuf.at[g, entry[1], c],
                     d_s.at[g * 16 + j], d_r.at[n], forward[entry])
            elif entry[2] == 0:
                q = entry[1]
                send(packed.at[pl.ds(base + (j + 1 - c) * 64, 64)], rbuf.at[g, q, c],
                     d_s.at[g * 16 + j], d_r.at[n], twin_dev)
                rbuf[g, q, c] = packed[pl.ds(base + (j + c) * 64, 64)]

    def rows_arrived(g, q):
        if q in (1, 2, 3):
            for s in range(2):
                n = number(g, q, s)
                arrived(rbuf.at[g, q, s], d_s.at[n], d_r.at[n], twin_dev)
            return
        n = number(g, q, 1 - c)
        arrived(rbuf.at[g, q, 1 - c], d_s.at[n], d_r.at[n], twin_dev)

    def couple(g, e):
        lines = pl.ds(e * 32, 32)
        left = rbuf[g, :, :, lines, :].reshape(512, modes)
        product = jnp.dot(left, wall[g * 2 + e], preferred_element_type=F32)
        res[g, :, :, lines, :] = product.astype(BF16).reshape(8, 2, 32, modes)

    def share(g, e):
        return pl.ds(e * 32, 32 if g else 64)

    def result_send(g, q, e=0):
        part_of = share(g, e)
        for s in range(2):
            if q == 0 and s == 1:
                first = g * 1024 + c * 64 + e * 32
                ret[pl.ds(first, part_of.size)] = res[g, 0, c, part_of]
                continue
            core = 1 - c if q == 0 else s
            sent, got = number(g + e, q, s), number(g + e, q, 0 if q == 0 else c)
            send(res.at[g, q, core, part_of], block(ret, g, q, c).at[part_of], b_s.at[sent], b_r.at[got],
                 twin_dev if q == 0 else source(q, s))

    def result_arrived(g, q, e=0):
        part_of = share(g, e)
        for s in range(1 if q == 0 else 2):
            n = number(g + e, q, s)
            core, dev = (1 - c, twin_dev) if q == 0 else (s, reach(q, s))
            arrived(block(ret, g, q, core).at[part_of], b_s.at[n], b_r.at[n], dev)

    for k in (1, 0):
        for g in range(2):
            pack(g, k)
    relay(1)
    for k in (2, 3, 4):
        for i in range(CHUNKS):
            arrived(wide.at[k - 2, part(i)], cast_s.at[0, i], cast_r.at[k - 2, i], beside[k - 1])
        for g in range(2):
            pack(g, k)
        if k == 2:
            relay(2)
    relay(3)
    for q in range(8):
        rows_arrived(0, q)
    order = (1, 2, 3, 4, 5, 6, 7, 0)
    couple(0, 0)
    couple(0, 1)
    for q in order:
        result_send(0, q)
    relay(4)
    for q in range(8):
        rows_arrived(1, q)
    for e in range(2):
        @pl.when(step == 3)
        def _():
            for n in range(e * PIECES, (e + 1) * PIECES):
                chain_arrived(n)
        couple(1, e)
        for q in order:
            result_send(1, q, e)
        if e == 0:
            relay(5)
    for q in range(8):
        result_arrived(0, q)
    acc[...] = jnp.dot(umat[0], ret[pl.ds(0, 1024)], preferred_element_type=F32)
    for q in range(4, 8):
        result_arrived(1, q, 0)
        result_arrived(1, q, 1)
    acc[...] += jnp.dot(umat[1, :, 512:], ret[pl.ds(1536, 512)], preferred_element_type=F32)
    for q in range(4):
        result_arrived(1, q, 0)
        result_arrived(1, q, 1)
    got = jnp.dot(umat[1, :, :512], ret[pl.ds(1024, 512)], preferred_element_type=F32)
    out_ref[...] = (acc[...] + got).astype(BF16)

    for copy in sends:
        copy.wait_send()
    for n in range(2 * PIECES):
        chain(n).wait_send()


def local(interface, owners, keep_proj, sibling_proj, coupling, pattern):
    rows, modes = interface.shape
    vmem = pl.BlockSpec(memory_space=pltpu.VMEM)
    dma = pltpu.SemaphoreType.DMA
    return pl.pallas_call(
        kernel,
        out_shape=pltpu.VMEM((rows, modes), BF16),
        in_specs=[pl.BlockSpec(memory_space=pltpu.HBM)] * 6,
        out_specs=vmem,
        scratch_shapes=[
            pltpu.VMEM((rows, modes), BF16),
            pltpu.VMEM((5, 1, rows), I32),
            pltpu.VMEM(keep_proj.shape, BF16),
            pltpu.VMEM(sibling_proj.shape, BF16),
            pltpu.VMEM(coupling.shape, BF16),
            pltpu.VMEM(pattern.shape, I32),
            dma((10,)),
            pltpu.VMEM((rows, modes), BF16),
            pltpu.VMEM((3, rows, modes), BF16),
        ]
        + [pltpu.VMEM((rows, modes), BF16)] * 6
        + [
            pltpu.VMEM((4, modes, modes), BF16),
            pltpu.VMEM((2 * rows, modes), BF16),
            pltpu.VMEM((2, 8, 2, 64, modes), BF16),
            pltpu.VMEM((2, 8, 2, 64, modes), BF16),
            pltpu.VMEM((2 * rows, modes), BF16),
            pltpu.VMEM((2, rows, rows), BF16),
            pltpu.VMEM((2, rows, rows), BF16),
            pltpu.VMEM((rows, modes), F32),
            pltpu.VMEM((5, 1, rows), I32),
            dma((4,)),
            dma((4,)),
            dma((3, CHUNKS)),
            dma((3, CHUNKS)),
        ]
        + [dma((CHUNKS,))] * 6
        + [dma((2 * PIECES,))] * 2
        + [dma((1,))] * 2
        + [dma((32,))] * 2
        + [dma((48,))] * 2,
        compiler_params=pltpu.CompilerParams(
            collective_id=0, has_side_effects=True, vmem_limit_bytes=56 << 20),
        name="condense",
    )(interface, owners.reshape(1, rows), keep_proj, sibling_proj, coupling, pattern)


def solution(mesh):
    in_specs = (
        P(("leaf", "blk"), None),
        P(("leaf", "blk"), None),
        P(),
        P(),
        P("leaf", None, None),
        P("leaf", None, None),
    )
    out_specs = P(("leaf", "blk"), None)
    return jax.shard_map(local, mesh=mesh, in_specs=in_specs, out_specs=out_specs, check_vma=False)
```

```python
import jax
import jax.numpy as jnp
from jax import lax
from jax.experimental import pallas as pl
from jax.experimental.pallas import tpu as pltpu
from jax.sharding import PartitionSpec as P

BS = 64
LEVELS = 3
EPS = 1e-06
SIZES = (128, 128, 128, 128, 128, 128, 128, 64, 64)
CHUNKS = len(SIZES)
PIECES = 4
RELAY = (
    ((0, 1), (), ()),
    ((2, 3), (0, 1), ()),
    ((4, 5), (2, 3), (0, 1)),
    ((6, 7), (4, 5), (2, 3)),
    ((), (6, 7), (4, 5)),
    ((), (), (6, 7)),
)
F32, BF16, I32 = jnp.float32, jnp.bfloat16, jnp.int32


REACH = (
    ((0, 0), (0, 0)),
    ((2, 0), (0, 2)),
    ((1, 1), (-1, -1)),
    ((1, -1), (-1, 1)),
    ((1, 0), (1, 0)),
    ((-1, 0), (-1, 0)),
    ((0, 1), (0, 1)),
    ((0, -1), (0, -1)),
)
SHARED = (
    (1, 2, 0), (1, 3, 0), (1, 1, 0), (1, 4, 0), (1, 4, 1), (0, 0, 0), (0, 0, 1),
    (2, 2, 1), (2, 3, 1), (2, 5, 0), (2, 5, 1), (3, 6, 0), (3, 6, 1),
)
BLOCKS = (
    SHARED + ((3, 1, 1), (4, 7, 0), (4, 7, 1)),
    SHARED + ((4, 7, 0), (4, 7, 1), (4, 1, 1)),
)


def leaf_of(y, x, zh, c):
    return ((lax.rem(y + 4, 4) * 4 + lax.rem(x + 4, 4)) * 2 + zh) * 2 + c


def kernel(x_hbm, own_hbm, keep_hbm, sib_hbm, coup_hbm, pat_hbm, out_ref,
           x_ref, own_all, keep, sib, coup, pat, load_s, cur3x, wide, twin, cur1, far, cur2, side, cur3, wall, packed, rbuf, res, ret, pmat, umat, acc, pos, own_s, own_r, cast_s, cast_r,
           twin_s, twin_r, far_s, far_r, side_s, side_r, zc_s, zc_r, g_s, g_r, d_s, d_r, b_s, b_r):
    rows, modes = x_hbm.shape
    leaf, zl = lax.axis_index("leaf"), lax.axis_index("blk")
    c, zh = lax.rem(leaf, 2), lax.rem(leaf // 2, 2)
    x, y = lax.rem(leaf // 4, 4), leaf // 16
    z = zh * 4 + zl

    def at(dx=0, dy=0, core=None):
        return (leaf_of(y + dy, x + dx, zh, c if core is None else core), zl)

    def at_z(dz):
        t = lax.rem(z + dz + 8, 8)
        return (leaf_of(y, x, t // 4, c), lax.rem(t, 4))

    twin_dev = at(core=1 - c)
    far_dev = at_z(4)
    hot = 1 - 2 * lax.rem(x, 2)
    side_dev = at(dx=hot)
    beside = (side_dev, at(dx=-hot), at(dy=-1), at(dy=1))
    pair_dev = at(2, 2)
    peers = [twin_dev, far_dev, at_z(1), at_z(-1), pair_dev]
    near = ((2, 0), (0, 2), (1, 1), (-1, -1), (-1, 1), (1, -1), (1, 0), (-1, 0), (0, 1), (0, -1))
    peers += [at(dx, dy, s) for dx, dy in near for s in range(2)]

    barrier = pltpu.get_barrier_semaphore()
    for peer in peers:
        pl.semaphore_signal(barrier, inc=1, device_id=peer, device_id_type=pl.DeviceIdType.MESH)

    loads = {}

    def load(name, src, dst):
        loads[name] = pltpu.make_async_copy(src, dst, load_s.at[len(loads)])
        loads[name].start()

    load("x", x_hbm, x_ref)
    load("keep0", keep_hbm.at[0], keep.at[0])
    load("sib0", sib_hbm.at[0], sib.at[0])
    load("coup", coup_hbm, coup)
    load("pat", pat_hbm, pat)
    load("own", own_hbm, own_all.at[0])
    for l in (1, 2):
        load(f"keep{l}", keep_hbm.at[l], keep.at[l])
        load(f"sib{l}", sib_hbm.at[l], sib.at[l])
    pl.semaphore_wait(barrier, len(peers))

    sends = []

    def send(src, dst, ss, rs, dev):
        copy = pltpu.make_async_remote_copy(
            src_ref=src, dst_ref=dst, send_sem=ss, recv_sem=rs,
            device_id=dev, device_id_type=pl.DeviceIdType.MESH)
        copy.start()
        sends.append(copy)

    def arrived(dst, ss, rs, dev):
        pltpu.make_async_remote_copy(
            src_ref=dst, dst_ref=dst, send_sem=ss, recv_sem=rs,
            device_id=dev, device_id_type=pl.DeviceIdType.MESH).wait_recv()

    def part(i):
        return pl.ds(sum(SIZES[:i]), SIZES[i])

    for i in range(CHUNKS):
        send(x_hbm.at[part(i)], twin.at[part(i)], twin_s.at[i], twin_r.at[i], twin_dev)

    def level(l, mine_ref, other_ref, dst, i):
        total = jnp.dot(mine_ref[part(i)], keep[l], preferred_element_type=F32)
        total = total + jnp.dot(other_ref[part(i)], sib[l], preferred_element_type=F32)
        scale = lax.rsqrt(jnp.mean(total * total, axis=1, keepdims=True) + EPS)
        dst[part(i)] = (total * scale).astype(BF16)

    def far_send(i):
        send(cur1.at[part(i)], far.at[part(i)], far_s.at[i], far_r.at[i], far_dev)

    for name in ("x", "keep0", "sib0"):
        loads[name].wait()
    for i in range(CHUNKS):
        arrived(twin.at[part(i)], twin_s.at[i], twin_r.at[i], twin_dev)
        level(0, x_ref, twin, cur1, i)
        far_send(i)

    loads["own"].wait()
    for n, slot in enumerate((1, 2, 4, 3)):
        send(own_all.at[0], own_all.at[slot], own_s.at[n], own_r.at[slot - 1], beside[n])

    loads["coup"].wait()
    loads["pat"].wait()
    grid_r = lax.broadcasted_iota(I32, (modes, 8), 0) // BS
    grid_c = lax.broadcasted_iota(I32, (modes, 8), 1)
    spread = (grid_r == grid_c).astype(F32).astype(BF16)
    wide_r = lax.broadcasted_iota(I32, (8, modes), 0)
    wide_c = lax.broadcasted_iota(I32, (8, modes), 1) // BS
    spread_t = (wide_r == wide_c).astype(F32).astype(BF16)
    half = jnp.dot(spread, pat[0].astype(F32).astype(BF16), preferred_element_type=F32).astype(BF16)
    mask = jnp.dot(half, spread_t, preferred_element_type=F32).astype(BF16)
    upper = y // 2
    wall[upper] = coup[0] * mask
    send(wall.at[upper], wall.at[upper], g_s.at[0], g_r.at[0], pair_dev)

    up = 1 - 2 * c
    step = jnp.where(c == 0, zl, 3 - zl)
    next_dev, prev_dev = at_z(up), at_z(-up)
    deep = modes // PIECES

    def chain(n):
        col, p = n // PIECES, n % PIECES
        piece = pl.ds(p * deep, deep)
        return pltpu.make_async_remote_copy(
            src_ref=wall.at[jnp.where(step == 3, 0, 2) + col, piece], dst_ref=wall.at[2 + col, piece],
            send_sem=zc_s.at[n], recv_sem=zc_r.at[n],
            device_id=next_dev, device_id_type=pl.DeviceIdType.MESH)

    def chain_arrived(n):
        arrived(wall.at[2 + n // PIECES, pl.ds(n % PIECES * deep, deep)], zc_s.at[n], zc_r.at[n], prev_dev)

    def base_of(o, home_x, home_y, towards):
        oc, ozh, ox, oy = o & 1, (o >> 1) & 1, (o >> 2) & 3, o >> 4
        dy = (oy - home_y) & 3
        dx = (towards * (ox - home_x) + (dy & 2)) & 3
        dy = dy & 1
        q = ((dx + dy) & 1) * 4 + dy * 2 + (dx >> 1)
        return ((((ozh ^ zh) * 8 + q) * 2 + oc) * 2 + (oy >> 1)) * 32

    homes = ((x, y, hot), (x + hot, y, -hot), (x - hot, y, -hot), (x, y - 1, hot), (x, y + 1, hot))
    tri_r = lax.broadcasted_iota(I32, (rows, rows), 0)
    tri_c = lax.broadcasted_iota(I32, (rows, rows), 1)

    def prepare(n):
        if n == 0:
            umat[0] = (tri_r < tri_c).astype(F32).astype(BF16)
            for k in range(5):
                if k:
                    arrived(own_all.at[k], own_s.at[k - 1], own_r.at[k - 1], beside[k - 1])
                mine = own_all[k]
                named = (mine == lax.broadcasted_iota(I32, (64, rows), 0)).astype(F32)
                rank = jnp.dot(named.astype(BF16), umat[0], preferred_element_type=F32)
                rank = jnp.sum(rank * named, axis=0, keepdims=True)
                pos[k] = base_of(mine, *homes[k]) + rank.astype(I32)
        elif n < 3:
            g = n - 1
            line = lax.broadcasted_iota(I32, (64, rows), 0)
            for j, (k, q, core) in enumerate(BLOCKS[g]):
                first = ((g * 8 + q) * 2 + core) * 64
                pmat[g, pl.ds(j * 64, 64), :] = (line + first == pos[k]).astype(F32).astype(BF16)
        else:
            line = jnp.where(tri_r == tri_c, pos[0], 0)
            column = jnp.sum(line.astype(F32), axis=1, keepdims=True).astype(I32)
            umat[n - 3] = (tri_c + (n - 3) * rows == column).astype(F32).astype(BF16)

    for name in ("keep1", "sib1", "keep2", "sib2"):
        loads[name].wait()

    def level2(i):
        arrived(side.at[part(i)], side_s.at[i], side_r.at[i], side_dev)
        level(2, cur2, side, cur3, i)
        for n, slot in enumerate((0, 2, 1)):
            send(cur3.at[part(i)], wide.at[slot, part(i)], cast_s.at[n, i], cast_r.at[slot, i], beside[n + 1])
        level(2, side, cur2, cur3x, i)

    def hand_on(pieces):
        for n in pieces:
            chain_arrived(n)
            chain(n).start()

    def relay(point):
        for place, pieces in enumerate(RELAY[point]):
            if pieces:
                pl.when(step == place)(lambda pieces=pieces: hand_on(pieces))

    for i in range(CHUNKS):
        arrived(far.at[part(i)], far_s.at[i], far_r.at[i], far_dev)
        if i == CHUNKS - 2:
            arrived(wall.at[1 - upper], g_s.at[0], g_r.at[0], pair_dev)

            @pl.when(step == 3)
            def _():
                for n in range(2 * PIECES):
                    chain(n).start()
        level(1, cur1, far, cur2, i)
        send(cur2.at[part(i)], side.at[part(i)], side_s.at[i], side_r.at[i], side_dev)
        if i:
            level2(i - 1)
        if i < 5:
            prepare(i)
    level2(CHUNKS - 1)
    relay(0)

    def block(ref, g, q, core):
        return ref.at[pl.ds(((g * 8 + q) * 2 + core) * 64, 64)]

    def reach(q, s):
        dx, dy = REACH[q][s]
        return at(dx * hot, dy, s)

    def source(q, s):
        (dx, dy), (ex, ey) = REACH[q]
        return at(jnp.where(c == 0, dx, ex) * hot, jnp.where(c == 0, -dy, -ey), s)

    def number(g, q, s):
        return (g * 8 + q) * 2 + s

    forward = {
        (1, 2, 0): at(0, 1, 0), (1, 3, 0): at(0, -1, 0), (1, 1, 0): at(-hot, 0, 0),
        (2, 2, 1): at(0, -1, 1), (2, 3, 1): at(0, 1, 1), (3, 1, 1): at(0, 1, 1), (4, 1, 1): at(0, -1, 1),
    }

    def pack(g, k):
        places = [j for j, entry in enumerate(BLOCKS[g]) if entry[0] == k]
        rows_of = cur3 if k == 0 else cur3x if k == 1 else wide.at[k - 2]
        span = pl.ds(places[0] * 64, len(places) * 64)
        base = g * 1024
        packed[pl.ds(base + places[0] * 64, len(places) * 64)] = jnp.dot(
            pmat[g, span, :], rows_of[...], preferred_element_type=F32).astype(BF16)
        for j in places:
            entry = BLOCKS[g][j]
            n = number(g, entry[1], c)
            if entry in forward:
                send(packed.at[pl.ds(base + j * 64, 64)], rbuf.at[g, entry[1], c],
                     d_s.at[g * 16 + j], d_r.at[n], forward[entry])
            elif entry[2] == 0:
                q = entry[1]
                send(packed.at[pl.ds(base + (j + 1 - c) * 64, 64)], rbuf.at[g, q, c],
                     d_s.at[g * 16 + j], d_r.at[n], twin_dev)
                rbuf[g, q, c] = packed[pl.ds(base + (j + c) * 64, 64)]

    def rows_arrived(g, q):
        if q in (1, 2, 3):
            for s in range(2):
                n = number(g, q, s)
                arrived(rbuf.at[g, q, s], d_s.at[n], d_r.at[n], twin_dev)
            return
        n = number(g, q, 1 - c)
        arrived(rbuf.at[g, q, 1 - c], d_s.at[n], d_r.at[n], twin_dev)

    def couple(g, e):
        lines = pl.ds(e * 32, 32)
        left = rbuf[g, :, :, lines, :].reshape(512, modes)
        product = jnp.dot(left, wall[g * 2 + e], preferred_element_type=F32)
        res[g, :, :, lines, :] = product.astype(BF16).reshape(8, 2, 32, modes)

    def share(g, e):
        return pl.ds(e * 32, 32 if g else 64)

    def result_send(g, q, e=0):
        part_of = share(g, e)
        for s in range(2):
            if q == 0 and s == 1:
                first = g * 1024 + c * 64 + e * 32
                ret[pl.ds(first, part_of.size)] = res[g, 0, c, part_of]
                continue
            core = 1 - c if q == 0 else s
            sent, got = number(g + e, q, s), number(g + e, q, 0 if q == 0 else c)
            send(res.at[g, q, core, part_of], block(ret, g, q, c).at[part_of], b_s.at[sent], b_r.at[got],
                 twin_dev if q == 0 else source(q, s))

    def result_arrived(g, q, e=0):
        part_of = share(g, e)
        for s in range(1 if q == 0 else 2):
            n = number(g + e, q, s)
            core, dev = (1 - c, twin_dev) if q == 0 else (s, reach(q, s))
            arrived(block(ret, g, q, core).at[part_of], b_s.at[n], b_r.at[n], dev)

    for k in (1, 0):
        for g in range(2):
            pack(g, k)
    relay(1)
    for k in (2, 3, 4):
        for i in range(CHUNKS):
            arrived(wide.at[k - 2, part(i)], cast_s.at[0, i], cast_r.at[k - 2, i], beside[k - 1])
        for g in range(2):
            pack(g, k)
        if k == 2:
            relay(2)
    relay(3)
    for q in range(8):
        rows_arrived(0, q)
    order = (1, 2, 3, 4, 5, 6, 7, 0)
    couple(0, 0)
    couple(0, 1)
    for q in order:
        result_send(0, q)
    relay(4)
    for q in range(8):
        rows_arrived(1, q)
    for e in range(2):
        @pl.when(step == 3)
        def _():
            for n in range(e * PIECES, (e + 1) * PIECES):
                chain_arrived(n)
        couple(1, e)
        for q in order:
            result_send(1, q, e)
        if e == 0:
            relay(5)
    for q in range(8):
        result_arrived(0, q)
    acc[...] = jnp.dot(umat[0], ret[pl.ds(0, 1024)], preferred_element_type=F32)
    for q in range(4, 8):
        result_arrived(1, q, 0)
        result_arrived(1, q, 1)
    acc[...] += jnp.dot(umat[1, :, 512:], ret[pl.ds(1536, 512)], preferred_element_type=F32)
    for q in range(4):
        result_arrived(1, q, 0)
        result_arrived(1, q, 1)
    got = jnp.dot(umat[1, :, :512], ret[pl.ds(1024, 512)], preferred_element_type=F32)
    out_ref[...] = (acc[...] + got).astype(BF16)

    for copy in sends:
        copy.wait_send()
    for n in range(2 * PIECES):
        chain(n).wait_send()


def local(interface, owners, keep_proj, sibling_proj, coupling, pattern):
    rows, modes = interface.shape
    vmem = pl.BlockSpec(memory_space=pltpu.VMEM)
    dma = pltpu.SemaphoreType.DMA
    return pl.pallas_call(
        kernel,
        out_shape=pltpu.VMEM((rows, modes), BF16),
        in_specs=[pl.BlockSpec(memory_space=pltpu.HBM)] * 6,
        out_specs=vmem,
        scratch_shapes=[
            pltpu.VMEM((rows, modes), BF16),
            pltpu.VMEM((5, 1, rows), I32),
            pltpu.VMEM(keep_proj.shape, BF16),
            pltpu.VMEM(sibling_proj.shape, BF16),
            pltpu.VMEM(coupling.shape, BF16),
            pltpu.VMEM(pattern.shape, I32),
            dma((10,)),
            pltpu.VMEM((rows, modes), BF16),
            pltpu.VMEM((3, rows, modes), BF16),
        ]
        + [pltpu.VMEM((rows, modes), BF16)] * 6
        + [
            pltpu.VMEM((4, modes, modes), BF16),
            pltpu.VMEM((2 * rows, modes), BF16),
            pltpu.VMEM((2, 8, 2, 64, modes), BF16),
            pltpu.VMEM((2, 8, 2, 64, modes), BF16),
            pltpu.VMEM((2 * rows, modes), BF16),
            pltpu.VMEM((2, rows, rows), BF16),
            pltpu.VMEM((2, rows, rows), BF16),
            pltpu.VMEM((rows, modes), F32),
            pltpu.VMEM((5, 1, rows), I32),
            dma((4,)),
            dma((4,)),
            dma((3, CHUNKS)),
            dma((3, CHUNKS)),
        ]
        + [dma((CHUNKS,))] * 6
        + [dma((2 * PIECES,))] * 2
        + [dma((1,))] * 2
        + [dma((32,))] * 2
        + [dma((48,))] * 2,
        compiler_params=pltpu.CompilerParams(
            collective_id=0, has_side_effects=True, vmem_limit_bytes=56 << 20),
        name="condense",
    )(interface, owners.reshape(1, rows), keep_proj, sibling_proj, coupling, pattern)


def solution(mesh):
    in_specs = (
        P(("leaf", "blk"), None),
        P(("leaf", "blk"), None),
        P(),
        P(),
        P("leaf", None, None),
        P("leaf", None, None),
    )
    out_specs = P(("leaf", "blk"), None)
    return jax.shard_map(local, mesh=mesh, in_specs=in_specs, out_specs=out_specs, check_vma=False)
```

```python
import jax
import jax.numpy as jnp
from jax import lax
from jax.experimental import pallas as pl
from jax.experimental.pallas import tpu as pltpu
from jax.sharding import PartitionSpec as P

BS = 64
LEVELS = 3
EPS = 1e-06
SIZES = (64, 128, 128, 128, 128, 128, 128, 128, 64)
CHUNKS = len(SIZES)
PIECES = 4
RELAY = (
    ((0, 1), (), ()),
    ((2, 3), (0, 1), ()),
    ((4, 5), (2, 3), (0, 1)),
    ((6, 7), (4, 5), (2, 3)),
    ((), (6, 7), (4, 5)),
    ((), (), (6, 7)),
)
F32, BF16, I32 = jnp.float32, jnp.bfloat16, jnp.int32


REACH = (
    ((0, 0), (0, 0)),
    ((2, 0), (0, 2)),
    ((1, 1), (-1, -1)),
    ((1, -1), (-1, 1)),
    ((1, 0), (1, 0)),
    ((-1, 0), (-1, 0)),
    ((0, 1), (0, 1)),
    ((0, -1), (0, -1)),
)
SHARED = (
    (1, 2, 0), (1, 3, 0), (1, 1, 0), (1, 4, 0), (1, 4, 1), (0, 0, 0), (0, 0, 1),
    (2, 2, 1), (2, 3, 1), (2, 5, 0), (2, 5, 1), (3, 6, 0), (3, 6, 1),
)
BLOCKS = (
    SHARED + ((3, 1, 1), (4, 7, 0), (4, 7, 1)),
    SHARED + ((4, 7, 0), (4, 7, 1), (4, 1, 1)),
)


def leaf_of(y, x, zh, c):
    return ((lax.rem(y + 4, 4) * 4 + lax.rem(x + 4, 4)) * 2 + zh) * 2 + c


def kernel(x_hbm, own_hbm, keep_hbm, sib_hbm, coup_hbm, pat_hbm, out_ref,
           x_ref, own_all, keep, sib, coup, pat, load_s, cur3x, wide, twin, cur1, far, cur2, side, cur3, wall, packed, rbuf, res, ret, pmat, umat, acc, pos, own_s, own_r, cast_s, cast_r,
           twin_s, twin_r, far_s, far_r, side_s, side_r, zc_s, zc_r, g_s, g_r, d_s, d_r, b_s, b_r):
    rows, modes = x_hbm.shape
    leaf, zl = lax.axis_index("leaf"), lax.axis_index("blk")
    c, zh = lax.rem(leaf, 2), lax.rem(leaf // 2, 2)
    x, y = lax.rem(leaf // 4, 4), leaf // 16
    z = zh * 4 + zl

    def at(dx=0, dy=0, core=None):
        return (leaf_of(y + dy, x + dx, zh, c if core is None else core), zl)

    def at_z(dz):
        t = lax.rem(z + dz + 8, 8)
        return (leaf_of(y, x, t // 4, c), lax.rem(t, 4))

    twin_dev = at(core=1 - c)
    far_dev = at_z(4)
    hot = 1 - 2 * lax.rem(x, 2)
    side_dev = at(dx=hot)
    beside = (side_dev, at(dx=-hot), at(dy=-1), at(dy=1))
    pair_dev = at(2, 2)
    peers = [twin_dev, far_dev, at_z(1), at_z(-1), pair_dev]
    near = ((2, 0), (0, 2), (1, 1), (-1, -1), (-1, 1), (1, -1), (1, 0), (-1, 0), (0, 1), (0, -1))
    peers += [at(dx, dy, s) for dx, dy in near for s in range(2)]

    barrier = pltpu.get_barrier_semaphore()
    for peer in peers:
        pl.semaphore_signal(barrier, inc=1, device_id=peer, device_id_type=pl.DeviceIdType.MESH)

    loads = {}

    def load(name, src, dst):
        loads[name] = pltpu.make_async_copy(src, dst, load_s.at[len(loads)])
        loads[name].start()

    load("x", x_hbm, x_ref)
    load("keep0", keep_hbm.at[0], keep.at[0])
    load("sib0", sib_hbm.at[0], sib.at[0])
    load("coup", coup_hbm, coup)
    load("pat", pat_hbm, pat)
    load("own", own_hbm, own_all.at[0])
    for l in (1, 2):
        load(f"keep{l}", keep_hbm.at[l], keep.at[l])
        load(f"sib{l}", sib_hbm.at[l], sib.at[l])
    pl.semaphore_wait(barrier, len(peers))

    sends = []

    def send(src, dst, ss, rs, dev):
        copy = pltpu.make_async_remote_copy(
            src_ref=src, dst_ref=dst, send_sem=ss, recv_sem=rs,
            device_id=dev, device_id_type=pl.DeviceIdType.MESH)
        copy.start()
        sends.append(copy)

    def arrived(dst, ss, rs, dev):
        pltpu.make_async_remote_copy(
            src_ref=dst, dst_ref=dst, send_sem=ss, recv_sem=rs,
            device_id=dev, device_id_type=pl.DeviceIdType.MESH).wait_recv()

    def part(i):
        return pl.ds(sum(SIZES[:i]), SIZES[i])

    for i in range(CHUNKS):
        send(x_hbm.at[part(i)], twin.at[part(i)], twin_s.at[i], twin_r.at[i], twin_dev)

    def level(l, mine_ref, other_ref, dst, i):
        total = jnp.dot(mine_ref[part(i)], keep[l], preferred_element_type=F32)
        total = total + jnp.dot(other_ref[part(i)], sib[l], preferred_element_type=F32)
        scale = lax.rsqrt(jnp.mean(total * total, axis=1, keepdims=True) + EPS)
        dst[part(i)] = (total * scale).astype(BF16)

    def far_send(i):
        send(cur1.at[part(i)], far.at[part(i)], far_s.at[i], far_r.at[i], far_dev)

    for name in ("x", "keep0", "sib0"):
        loads[name].wait()
    for i in range(CHUNKS):
        arrived(twin.at[part(i)], twin_s.at[i], twin_r.at[i], twin_dev)
        level(0, x_ref, twin, cur1, i)
        far_send(i)

    loads["own"].wait()
    for n, slot in enumerate((1, 2, 4, 3)):
        send(own_all.at[0], own_all.at[slot], own_s.at[n], own_r.at[slot - 1], beside[n])

    loads["coup"].wait()
    loads["pat"].wait()
    grid_r = lax.broadcasted_iota(I32, (modes, 8), 0) // BS
    grid_c = lax.broadcasted_iota(I32, (modes, 8), 1)
    spread = (grid_r == grid_c).astype(F32).astype(BF16)
    wide_r = lax.broadcasted_iota(I32, (8, modes), 0)
    wide_c = lax.broadcasted_iota(I32, (8, modes), 1) // BS
    spread_t = (wide_r == wide_c).astype(F32).astype(BF16)
    half = jnp.dot(spread, pat[0].astype(F32).astype(BF16), preferred_element_type=F32).astype(BF16)
    mask = jnp.dot(half, spread_t, preferred_element_type=F32).astype(BF16)
    upper = y // 2
    wall[upper] = coup[0] * mask
    send(wall.at[upper], wall.at[upper], g_s.at[0], g_r.at[0], pair_dev)

    up = 1 - 2 * c
    step = jnp.where(c == 0, zl, 3 - zl)
    next_dev, prev_dev = at_z(up), at_z(-up)
    deep = modes // PIECES

    def chain(n):
        col, p = n // PIECES, n % PIECES
        piece = pl.ds(p * deep, deep)
        return pltpu.make_async_remote_copy(
            src_ref=wall.at[jnp.where(step == 3, 0, 2) + col, piece], dst_ref=wall.at[2 + col, piece],
            send_sem=zc_s.at[n], recv_sem=zc_r.at[n],
            device_id=next_dev, device_id_type=pl.DeviceIdType.MESH)

    def chain_arrived(n):
        arrived(wall.at[2 + n // PIECES, pl.ds(n % PIECES * deep, deep)], zc_s.at[n], zc_r.at[n], prev_dev)

    def base_of(o, home_x, home_y, towards):
        oc, ozh, ox, oy = o & 1, (o >> 1) & 1, (o >> 2) & 3, o >> 4
        dy = (oy - home_y) & 3
        dx = (towards * (ox - home_x) + (dy & 2)) & 3
        dy = dy & 1
        q = ((dx + dy) & 1) * 4 + dy * 2 + (dx >> 1)
        return ((((ozh ^ zh) * 8 + q) * 2 + oc) * 2 + (oy >> 1)) * 32

    homes = ((x, y, hot), (x + hot, y, -hot), (x - hot, y, -hot), (x, y - 1, hot), (x, y + 1, hot))
    tri_r = lax.broadcasted_iota(I32, (rows, rows), 0)
    tri_c = lax.broadcasted_iota(I32, (rows, rows), 1)

    def prepare(n):
        if n == 0:
            umat[0] = (tri_r < tri_c).astype(F32).astype(BF16)
            for k in range(5):
                if k:
                    arrived(own_all.at[k], own_s.at[k - 1], own_r.at[k - 1], beside[k - 1])
                mine = own_all[k]
                named = (mine == lax.broadcasted_iota(I32, (64, rows), 0)).astype(F32)
                rank = jnp.dot(named.astype(BF16), umat[0], preferred_element_type=F32)
                rank = jnp.sum(rank * named, axis=0, keepdims=True)
                pos[k] = base_of(mine, *homes[k]) + rank.astype(I32)
        elif n < 3:
            g = n - 1
            line = lax.broadcasted_iota(I32, (64, rows), 0)
            for j, (k, q, core) in enumerate(BLOCKS[g]):
                first = ((g * 8 + q) * 2 + core) * 64
                pmat[g, pl.ds(j * 64, 64), :] = (line + first == pos[k]).astype(F32).astype(BF16)
        else:
            line = jnp.where(tri_r == tri_c, pos[0], 0)
            column = jnp.sum(line.astype(F32), axis=1, keepdims=True).astype(I32)
            umat[n - 3] = (tri_c + (n - 3) * rows == column).astype(F32).astype(BF16)

    for name in ("keep1", "sib1", "keep2", "sib2"):
        loads[name].wait()

    def level2(i):
        arrived(side.at[part(i)], side_s.at[i], side_r.at[i], side_dev)
        level(2, cur2, side, cur3, i)
        for n, slot in enumerate((0, 2, 1)):
            send(cur3.at[part(i)], wide.at[slot, part(i)], cast_s.at[n, i], cast_r.at[slot, i], beside[n + 1])
        level(2, side, cur2, cur3x, i)

    def hand_on(pieces):
        for n in pieces:
            chain_arrived(n)
            chain(n).start()

    def relay(point):
        for place, pieces in enumerate(RELAY[point]):
            if pieces:
                pl.when(step == place)(lambda pieces=pieces: hand_on(pieces))

    for i in range(CHUNKS):
        arrived(far.at[part(i)], far_s.at[i], far_r.at[i], far_dev)
        if i == CHUNKS - 2:
            arrived(wall.at[1 - upper], g_s.at[0], g_r.at[0], pair_dev)

            @pl.when(step == 3)
            def _():
                for n in range(2 * PIECES):
                    chain(n).start()
        level(1, cur1, far, cur2, i)
        send(cur2.at[part(i)], side.at[part(i)], side_s.at[i], side_r.at[i], side_dev)
        if i:
            level2(i - 1)
        if i < 5:
            prepare(i)
    level2(CHUNKS - 1)
    relay(0)

    def block(ref, g, q, core):
        return ref.at[pl.ds(((g * 8 + q) * 2 + core) * 64, 64)]

    def reach(q, s):
        dx, dy = REACH[q][s]
        return at(dx * hot, dy, s)

    def source(q, s):
        (dx, dy), (ex, ey) = REACH[q]
        return at(jnp.where(c == 0, dx, ex) * hot, jnp.where(c == 0, -dy, -ey), s)

    def number(g, q, s):
        return (g * 8 + q) * 2 + s

    forward = {
        (1, 2, 0): at(0, 1, 0), (1, 3, 0): at(0, -1, 0), (1, 1, 0): at(-hot, 0, 0),
        (2, 2, 1): at(0, -1, 1), (2, 3, 1): at(0, 1, 1), (3, 1, 1): at(0, 1, 1), (4, 1, 1): at(0, -1, 1),
    }

    def pack(g, k):
        places = [j for j, entry in enumerate(BLOCKS[g]) if entry[0] == k]
        rows_of = cur3 if k == 0 else cur3x if k == 1 else wide.at[k - 2]
        span = pl.ds(places[0] * 64, len(places) * 64)
        base = g * 1024
        packed[pl.ds(base + places[0] * 64, len(places) * 64)] = jnp.dot(
            pmat[g, span, :], rows_of[...], preferred_element_type=F32).astype(BF16)
        for j in places:
            entry = BLOCKS[g][j]
            n = number(g, entry[1], c)
            if entry in forward:
                send(packed.at[pl.ds(base + j * 64, 64)], rbuf.at[g, entry[1], c],
                     d_s.at[g * 16 + j], d_r.at[n], forward[entry])
            elif entry[2] == 0:
                q = entry[1]
                send(packed.at[pl.ds(base + (j + 1 - c) * 64, 64)], rbuf.at[g, q, c],
                     d_s.at[g * 16 + j], d_r.at[n], twin_dev)
                rbuf[g, q, c] = packed[pl.ds(base + (j + c) * 64, 64)]

    def rows_arrived(g, q):
        if q in (1, 2, 3):
            for s in range(2):
                n = number(g, q, s)
                arrived(rbuf.at[g, q, s], d_s.at[n], d_r.at[n], twin_dev)
            return
        n = number(g, q, 1 - c)
        arrived(rbuf.at[g, q, 1 - c], d_s.at[n], d_r.at[n], twin_dev)

    def couple(g, e):
        lines = pl.ds(e * 32, 32)
        left = rbuf[g, :, :, lines, :].reshape(512, modes)
        product = jnp.dot(left, wall[g * 2 + e], preferred_element_type=F32)
        res[g, :, :, lines, :] = product.astype(BF16).reshape(8, 2, 32, modes)

    def share(g, e):
        return pl.ds(e * 32, 32 if g else 64)

    def result_send(g, q, e=0):
        part_of = share(g, e)
        for s in range(2):
            if q == 0 and s == 1:
                first = g * 1024 + c * 64 + e * 32
                ret[pl.ds(first, part_of.size)] = res[g, 0, c, part_of]
                continue
            core = 1 - c if q == 0 else s
            sent, got = number(g + e, q, s), number(g + e, q, 0 if q == 0 else c)
            send(res.at[g, q, core, part_of], block(ret, g, q, c).at[part_of], b_s.at[sent], b_r.at[got],
                 twin_dev if q == 0 else source(q, s))

    def result_arrived(g, q, e=0):
        part_of = share(g, e)
        for s in range(1 if q == 0 else 2):
            n = number(g + e, q, s)
            core, dev = (1 - c, twin_dev) if q == 0 else (s, reach(q, s))
            arrived(block(ret, g, q, core).at[part_of], b_s.at[n], b_r.at[n], dev)

    for k in (1, 0):
        for g in range(2):
            pack(g, k)
    relay(1)
    for k in (2, 3, 4):
        for i in range(CHUNKS):
            arrived(wide.at[k - 2, part(i)], cast_s.at[0, i], cast_r.at[k - 2, i], beside[k - 1])
        for g in range(2):
            pack(g, k)
        if k == 2:
            relay(2)
    relay(3)
    for q in range(8):
        rows_arrived(0, q)
    order = (1, 2, 3, 4, 5, 6, 7, 0)
    couple(0, 0)
    couple(0, 1)
    for q in order:
        result_send(0, q)
    relay(4)
    for q in range(8):
        rows_arrived(1, q)
    for e in range(2):
        @pl.when(step == 3)
        def _():
            for n in range(e * PIECES, (e + 1) * PIECES):
                chain_arrived(n)
        couple(1, e)
        for q in order:
            result_send(1, q, e)
        if e == 0:
            relay(5)
    for q in range(8):
        result_arrived(0, q)
    acc[...] = jnp.dot(umat[0], ret[pl.ds(0, 1024)], preferred_element_type=F32)
    for q in range(4, 8):
        result_arrived(1, q, 0)
        result_arrived(1, q, 1)
    acc[...] += jnp.dot(umat[1, :, 512:], ret[pl.ds(1536, 512)], preferred_element_type=F32)
    for q in range(4):
        result_arrived(1, q, 0)
        result_arrived(1, q, 1)
    got = jnp.dot(umat[1, :, :512], ret[pl.ds(1024, 512)], preferred_element_type=F32)
    out_ref[...] = (acc[...] + got).astype(BF16)

    for copy in sends:
        copy.wait_send()
    for n in range(2 * PIECES):
        chain(n).wait_send()


def local(interface, owners, keep_proj, sibling_proj, coupling, pattern):
    rows, modes = interface.shape
    vmem = pl.BlockSpec(memory_space=pltpu.VMEM)
    dma = pltpu.SemaphoreType.DMA
    return pl.pallas_call(
        kernel,
        out_shape=pltpu.VMEM((rows, modes), BF16),
        in_specs=[pl.BlockSpec(memory_space=pltpu.HBM)] * 6,
        out_specs=vmem,
        scratch_shapes=[
            pltpu.VMEM((rows, modes), BF16),
            pltpu.VMEM((5, 1, rows), I32),
            pltpu.VMEM(keep_proj.shape, BF16),
            pltpu.VMEM(sibling_proj.shape, BF16),
            pltpu.VMEM(coupling.shape, BF16),
            pltpu.VMEM(pattern.shape, I32),
            dma((10,)),
            pltpu.VMEM((rows, modes), BF16),
            pltpu.VMEM((3, rows, modes), BF16),
        ]
        + [pltpu.VMEM((rows, modes), BF16)] * 6
        + [
            pltpu.VMEM((4, modes, modes), BF16),
            pltpu.VMEM((2 * rows, modes), BF16),
            pltpu.VMEM((2, 8, 2, 64, modes), BF16),
            pltpu.VMEM((2, 8, 2, 64, modes), BF16),
            pltpu.VMEM((2 * rows, modes), BF16),
            pltpu.VMEM((2, rows, rows), BF16),
            pltpu.VMEM((2, rows, rows), BF16),
            pltpu.VMEM((rows, modes), F32),
            pltpu.VMEM((5, 1, rows), I32),
            dma((4,)),
            dma((4,)),
            dma((3, CHUNKS)),
            dma((3, CHUNKS)),
        ]
        + [dma((CHUNKS,))] * 6
        + [dma((2 * PIECES,))] * 2
        + [dma((1,))] * 2
        + [dma((32,))] * 2
        + [dma((48,))] * 2,
        compiler_params=pltpu.CompilerParams(
            collective_id=0, has_side_effects=True, vmem_limit_bytes=56 << 20),
        name="condense",
    )(interface, owners.reshape(1, rows), keep_proj, sibling_proj, coupling, pattern)


def solution(mesh):
    in_specs = (
        P(("leaf", "blk"), None),
        P(("leaf", "blk"), None),
        P(),
        P(),
        P("leaf", None, None),
        P("leaf", None, None),
    )
    out_specs = P(("leaf", "blk"), None)
    return jax.shard_map(local, mesh=mesh, in_specs=in_specs, out_specs=out_specs, check_vma=False)
```
